128 devices in a mesh: cell: 8 (over z_lo, x), gene: 16 (over z_hi, y, core).
Axes of the slice: x: 4, y: 4, z: 4 (z_hi: 2, z_lo: 2; z = z_hi * 2 + z_lo), core: 2. Of those that a mesh axis runs over, the one named last changes fastest.
Arguments:
- expression: bfloat16 [8192, 30720], P('cell', 'gene'), may hold values from -12 to 12
- prior_values: bfloat16 [30720, 1792], P('gene'), may hold values from -0.0625 to 0.0625
- block_mask: int32 [240, 14], P('gene'), may hold values 0 or 1
- gram_inverse: bfloat16 [1792, 1792], P(None, 'gene'), may hold values from -1 to 2
Outputs:
- coefficients: float32 [1792, 30720], P('cell', 'gene')
The draws below stay inside these ranges and needn't reach their ends.
All inputs are finite; a program needn't handle non-finite values. No bound on the sum of `block_mask` on one device may be relied on, other than what follows from the above.
Results may differ from the reference program's by a relative error of at most 0.025.
Values may be sent and summed in bfloat16 or wider, within the bound.
A program may use at most 128 MiB of HBM per device.

```python
import jax
import jax.numpy as jnp
from jax import lax

F = 1792
BLOCK = 128
CELL_DEV = 1024
ITERS = 2
CELLS = 8192
GENES = 30720
N_CELL = 8


def draw_gram_inverse(key, part):
    noise = jnp.clip(jax.random.normal(jax.random.fold_in(key, 17), (F, F), jnp.float32), -4.0, 4.0)
    matrix = jnp.eye(F, dtype=jnp.float32) + 0.5 * noise / jnp.sqrt(jnp.float32(F))
    return matrix.astype(jnp.bfloat16)


def draw_expression(key, part):
    position = (jnp.arange(CELLS, dtype=jnp.float32) + 0.5) / CELLS
    values = jnp.clip(jax.random.normal(jax.random.fold_in(key, 23), (CELLS, GENES), jnp.float32), -4.0, 4.0)
    row_scale = jnp.exp(jnp.log(8.0) * (position - 0.5))
    field = values * row_scale[:, None]
    return field.astype(jnp.bfloat16)


def touch_ends(entries, stream_key, least, largest):
    spot = [jax.random.randint(jax.random.fold_in(stream_key, axis), (), 0, length) for axis, length in enumerate(entries.shape)]
    main_axis = entries.shape.index(max(entries.shape))
    neighbour = spot[:main_axis] + [(spot[main_axis] + 1) % entries.shape[main_axis]] + spot[main_axis + 1:]
    return entries.at[tuple(spot)].set(least).at[tuple(neighbour)].set(largest)


def block_levels(stream_key, shape, split, low, top_value):
    factor_of = 1.0
    for dim, parts in split:
        heights = jax.random.uniform(jax.random.fold_in(jax.random.fold_in(stream_key, 6), dim), (parts,), jnp.float32, low / len(split), top_value / len(split))
        factor_of = factor_of * jnp.repeat(jnp.exp(heights), shape[dim] // parts).reshape((-1,) + (1,) * (len(shape) - 1 - dim))
    return factor_of


def gaussian(stream_key, dims, width, bound, pieces=(), held_as=jnp.bfloat16):
    loudness = block_levels(stream_key, dims, pieces, -0.22, 0.18) if pieces else 1.0
    drawn = jax.random.normal(stream_key, dims, jnp.float32) * width * loudness
    return jnp.minimum(jnp.maximum(drawn, -bound), bound).astype(held_as)


def setup_inputs(seed: int = 0) -> dict:
    key_of = jax.random.split(jax.random.key(seed), 5)
    expression = draw_expression(jax.random.fold_in(key_of[4], 71), 0)
    prior_values = gaussian(key_of[1], (GENES, F), (GENES // 3) ** -0.5, 0.0625, ((0, 16),))
    block_mask = touch_ends((jax.random.randint(key_of[2], (GENES // BLOCK, F // BLOCK), 0, 3) < 1).astype(jnp.int32), jax.random.fold_in(key_of[2], 1), 0, 1)
    gram_inverse = draw_gram_inverse(jax.random.fold_in(key_of[4], 71), 0)
    return {"expression": expression, "prior_values": prior_values, "block_mask": block_mask, "gram_inverse": gram_inverse}


OUT_UNITS = 100.0
LASSO = 0.006
RIDGE = 0.1
PRIOR_RELIEF = 0.7
EPSILON = 1e-6


def shrink(moved, limit, step_size):
    kept = jnp.maximum(moved - limit, 0.0) - jnp.maximum(-moved - limit, 0.0)
    return kept / (1.0 + step_size * RIDGE)


def reference(expression, prior_values, block_mask, gram_inverse):
    support = jnp.repeat(jnp.repeat(block_mask.astype(jnp.float32), BLOCK, axis=0), BLOCK, axis=1)
    masked = (prior_values.astype(jnp.float32) * support).astype(jnp.bfloat16)
    tf_scores = jnp.dot(expression, masked, preferred_element_type=jnp.float32).astype(jnp.bfloat16)
    activity = jnp.dot(tf_scores, gram_inverse, preferred_element_type=jnp.float32).astype(jnp.bfloat16)
    widened = activity.astype(jnp.float32)
    sum_squares = jnp.sum(widened * widened)
    step_size = 0.5 / (sum_squares / (CELLS * F) + EPSILON)
    limit = step_size * LASSO * (1.0 - PRIOR_RELIEF * support.T)
    coefficient = jnp.zeros((F, GENES), jnp.float32)
    blocked_activity = activity.reshape(N_CELL, CELL_DEV, F)

    def add_block(carried, pair):
        product = jnp.dot(pair[0].T, pair[1], preferred_element_type=jnp.float32)
        rounded = lax.optimization_barrier(product.astype(jnp.bfloat16))
        return carried + rounded.astype(jnp.float32), None

    for sweep in range(ITERS):
        if sweep == 0:
            residual = -expression
        else:
            fitted = jnp.dot(activity, coefficient.astype(jnp.bfloat16), preferred_element_type=jnp.float32)
            residual = (fitted - expression.astype(jnp.float32)).astype(jnp.bfloat16)
        blocked_residual = residual.reshape(N_CELL, CELL_DEV, GENES)
        summed, unused = lax.scan(add_block, jnp.zeros((F, GENES), jnp.float32), (blocked_activity, blocked_residual))
        gradient = summed / CELLS
        coefficient = shrink(coefficient - step_size * gradient, limit, step_size)
    return coefficient * OUT_UNITS
```

```python
import jax
import jax.numpy as jnp
from jax import lax
from jax.sharding import PartitionSpec as P

BLOCK = 128

OUT_UNITS = 100.0
LASSO = 0.006
RIDGE = 0.1
PRIOR_RELIEF = 0.7
EPSILON = 1e-06


def shrink(moved, limit, step_size):
    kept = jnp.maximum(moved - limit, 0.0) - jnp.maximum(-moved - limit, 0.0)
    return kept / (1.0 + step_size * RIDGE)


def on_device(expression, prior_values, block_mask, gram_inverse):
    cell_devices = lax.axis_size("cell")
    cell_rows, gene_rows = expression.shape
    tf_total = prior_values.shape[1]
    gene_blocks, tf_blocks = block_mask.shape
    support = block_mask.astype(jnp.bfloat16)[:, None, :, None]
    masked = (prior_values.reshape(gene_blocks, BLOCK, tf_blocks, BLOCK) * support).reshape(
        gene_rows, tf_total
    )
    tf_scores = lax.psum_scatter(
        lax.dot_general(
            masked, expression, (((0,), (1,)), ((), ())), preferred_element_type=jnp.float32
        ).astype(jnp.bfloat16),
        "gene",
        scatter_dimension=0,
        tiled=True,
    )
    activity_part = lax.dot_general(
        gram_inverse,
        lax.all_gather(tf_scores, "gene", axis=0, tiled=True),
        (((0,), (0,)), ((), ())),
        preferred_element_type=jnp.float32,
    ).astype(jnp.bfloat16)
    activity_t = lax.all_gather(activity_part, "gene", axis=0, tiled=True)
    widened = activity_t.astype(jnp.float32)
    sum_squares = lax.psum(jnp.sum(widened * widened), "cell")
    total_cells = cell_rows * cell_devices
    step_size = 0.5 / (sum_squares / (total_cells * tf_total) + EPSILON)
    tf_rows = tf_total // cell_devices
    first_row = lax.axis_index("cell") * tf_rows
    relief = block_mask.T.astype(jnp.float32)[:, None, :, None]
    penalty = jnp.broadcast_to(1.0 - PRIOR_RELIEF * relief, (tf_blocks, BLOCK, gene_blocks, BLOCK))
    penalty = lax.dynamic_slice_in_dim(penalty.reshape(tf_total, gene_rows), first_row, tf_rows, 0)
    limit = step_size * LASSO * penalty

    gram_part = lax.dot_general(
        activity_t,
        activity_part,
        (((1,), (1,)), ((), ())),
        preferred_element_type=jnp.float32,
    ).astype(jnp.bfloat16)
    first_term = jnp.dot(activity_t, expression, preferred_element_type=jnp.float32)
    first = lax.psum_scatter(
        first_term.astype(jnp.bfloat16), "cell", scatter_dimension=0, tiled=True
    ).astype(jnp.float32)
    gram_rows = lax.all_gather(
        lax.psum_scatter(gram_part, "cell", scatter_dimension=0, tiled=True),
        "gene",
        axis=1,
        tiled=True,
    )
    scale = step_size / total_cells
    coefficient = shrink(scale * first, limit, step_size)
    whole = lax.all_gather(coefficient.astype(jnp.bfloat16), "cell", axis=0, tiled=True)
    second = jnp.dot(gram_rows, whole, preferred_element_type=jnp.float32)
    coefficient = shrink(coefficient - scale * (second - first), limit, step_size)
    return coefficient * OUT_UNITS


def solution(mesh):
    in_specs = (P("cell", "gene"), P("gene", None), P("gene", None), P(None, "gene"))
    out_specs = P("cell", "gene")
    return jax.shard_map(
        on_device, mesh=mesh, in_specs=in_specs, out_specs=out_specs, check_vma=False
    )
```

```python
import functools

import jax
import jax.numpy as jnp
from jax import lax
from jax.experimental import pallas as pl
from jax.experimental.pallas import tpu as pltpu
from jax.sharding import PartitionSpec as P

BLOCK = 128

OUT_UNITS = 100.0
LASSO = 0.006
RIDGE = 0.1
PRIOR_RELIEF = 0.7
EPSILON = 1e-06

MESH = pl.DeviceIdType.MESH
CHIPS = 8
CHUNK = 256
OFFSETS = ((0, 1), (0, 3), (1, 0), (0, 2), (1, 1), (1, 3), (1, 2))


def shrink(moved, limit, step_size):
    kept = jnp.maximum(moved - limit, 0.0) - jnp.maximum(-moved - limit, 0.0)
    return kept / (1.0 + step_size * RIDGE)


def activity_kernel(
    x_hbm, prior_hbm, support_ref, gram_ref, at_ref,
    x, prior, part, pair, total, got, scores, acc,
    x_sem, prior_sem, pair_send, pair_recv, rs_send, rs_recv,
    ag_send, ag_recv, fw_send, fw_recv, at_send, at_recv, af_send, af_recv,
):
    chunks = prior.shape[0]
    me = lax.axis_index("gene")
    core = me % 2
    chip = me // 2
    y, z = chip % 4, chip // 4
    partner = chip * 2 + (1 - core)
    others = [((z + dz) % 2) * 4 + (y + dy) % 4 for dz, dy in OFFSETS]

    x_copy = pltpu.make_async_copy(x_hbm, x, x_sem)
    x_copy.start()

    def prior_copy(n):
        columns = pl.ds(pl.multiple_of(n * CHUNK, CHUNK), CHUNK)
        return pltpu.make_async_copy(prior_hbm.at[:, columns], prior.at[n], prior_sem.at[n])

    for n in range(chunks):
        prior_copy(n).start()

    barrier = pltpu.get_barrier_semaphore()
    for device in [other * 2 + core for other in others] + [partner]:
        pl.semaphore_signal(barrier, inc=1, device_id={"gene": device}, device_id_type=MESH)
    pl.semaphore_wait(barrier, len(others) + 1)

    def remote(src, dst, send, recv, device):
        return pltpu.make_async_remote_copy(
            src_ref=src, dst_ref=dst, send_sem=send, recv_sem=recv,
            device_id={"gene": device}, device_id_type=MESH,
        )

    def pair_copy(n):
        return remote(
            part.at[n, :, 1 - core], pair.at[n], pair_send.at[n], pair_recv.at[n], partner
        )

    def rs_copy(n, o, slot):
        return remote(
            total.at[n, others[o]], got.at[n, slot], rs_send.at[n, o], rs_recv.at[n, slot],
            others[o] * 2 + core,
        )

    def ag_copy(n, o, slot):
        block = scores.at[n, slot, core]
        return remote(block, block, ag_send.at[n, o], ag_recv.at[n, slot], others[o] * 2 + core)

    def fw_copy(n, slot, side):
        block = scores.at[n, slot, side]
        return remote(block, block, fw_send.at[n, slot], fw_recv.at[n, slot], partner)

    def at_copy(o, slot):
        block = at_ref.at[slot * 2 + core]
        return remote(block, block, at_send.at[o], at_recv.at[slot], others[o] * 2 + core)

    def af_copy(slot, side):
        block = at_ref.at[slot * 2 + side]
        return remote(block, block, af_send.at[slot], af_recv.at[slot], partner)

    x_copy.wait()

    def spread(n):
        pair_copy(n).wait_recv()
        own = part[n, :, core].astype(jnp.float32)
        total[n] = (own + pair[n].astype(jnp.float32)).astype(jnp.bfloat16)
        for o in range(len(others)):
            rs_copy(n, o, chip).start()

    def multiply(n, carry):
        prior_copy(n).wait()
        masked = prior[n].reshape(-1, BLOCK // 16, 16, CHUNK) * support_ref[n][:, None]
        prior[n] = masked.reshape(prior.shape[1:])
        product = jnp.dot(x[...], prior[n], preferred_element_type=jnp.float32)
        part[n] = product.astype(jnp.bfloat16).reshape(part.shape[1:])
        pair_copy(n).start()

        @pl.when(n > 0)
        def _():
            spread(n - 1)

        return carry

    lax.fori_loop(0, chunks, multiply, 0)
    spread(chunks - 1)

    def collect(n, carry):
        value = total[n, chip].astype(jnp.float32)
        for o in range(len(others)):
            rs_copy(n, o, others[o]).wait_recv()
            value = value + got[n, others[o]].astype(jnp.float32)
        scores[n, chip, core] = value.astype(jnp.bfloat16)
        for o in range(len(others)):
            ag_copy(n, o, chip).start()
        fw_copy(n, chip, core).start()
        return carry

    lax.fori_loop(0, chunks, collect, 0)

    def forward(n, carry):
        for o in range(len(others)):
            ag_copy(n, o, others[o]).wait_recv()
            fw_copy(n, others[o], core).start()
        return carry

    lax.fori_loop(0, chunks, forward, 0)

    acc[...] = jnp.zeros_like(acc)

    def mix(n, carry):
        for slot in range(CHIPS):
            fw_copy(n, slot, 1 - core).wait_recv()
        acc[...] += lax.dot_general(
            gram_ref[n], scores[n].reshape(-1, CHUNK), (((1,), (1,)), ((), ())),
            preferred_element_type=jnp.float32,
        )
        return carry

    lax.fori_loop(0, chunks, mix, 0)
    at_ref[me] = acc[...].astype(jnp.bfloat16)
    for o in range(len(others)):
        at_copy(o, chip).start()
    af_copy(chip, core).start()
    for o in range(len(others)):
        at_copy(o, others[o]).wait_recv()
        af_copy(others[o], core).start()
    for slot in range(CHIPS):
        af_copy(slot, 1 - core).wait_recv()

    def drain(n, carry):
        pair_copy(n).wait_send()
        for o in range(len(others)):
            rs_copy(n, o, chip).wait_send()
            ag_copy(n, o, chip).wait_send()
        for slot in range(CHIPS):
            fw_copy(n, slot, core).wait_send()
        return carry

    lax.fori_loop(0, chunks, drain, 0)
    for o in range(len(others)):
        at_copy(o, chip).wait_send()
    for slot in range(CHIPS):
        af_copy(slot, core).wait_send()


def activity_of(expression, prior_values, block_mask, gram_inverse):
    devices = lax.axis_size("gene")
    cells, genes = expression.shape
    factors = prior_values.shape[1]
    own = gram_inverse.shape[1]
    chunks = factors // CHUNK
    rows = cells // devices
    support = jnp.repeat(block_mask.astype(jnp.bfloat16), BLOCK, axis=1)
    support = support.reshape(genes // BLOCK, chunks, 1, CHUNK).transpose(1, 0, 2, 3)
    support = jnp.broadcast_to(support, (chunks, genes // BLOCK, 16, CHUNK))
    gram = gram_inverse.T.reshape(own, chunks, CHUNK).transpose(1, 0, 2)
    bf = jnp.bfloat16
    dma = pltpu.SemaphoreType.DMA
    links = len(OFFSETS)
    return pl.pallas_call(
        activity_kernel,
        out_shape=jax.ShapeDtypeStruct((devices, own, cells), bf),
        in_specs=[pl.BlockSpec(memory_space=pl.ANY)] * 2
        + [pl.BlockSpec(memory_space=pltpu.VMEM)] * 2,
        out_specs=pl.BlockSpec(memory_space=pltpu.VMEM),
        scratch_shapes=[
            pltpu.VMEM((cells, genes), bf),
            pltpu.VMEM((chunks, genes, CHUNK), bf),
            pltpu.VMEM((chunks, CHIPS, 2, rows, CHUNK), bf),
            pltpu.VMEM((chunks, CHIPS, rows, CHUNK), bf),
            pltpu.VMEM((chunks, CHIPS, rows, CHUNK), bf),
            pltpu.VMEM((chunks, CHIPS, rows, CHUNK), bf),
            pltpu.VMEM((chunks, CHIPS, 2, rows, CHUNK), bf),
            pltpu.VMEM((own, cells), jnp.float32),
            dma, dma((chunks,)), dma((chunks,)), dma((chunks,)),
            dma((chunks, links)), dma((chunks, CHIPS)),
            dma((chunks, links)), dma((chunks, CHIPS)),
            dma((chunks, CHIPS)), dma((chunks, CHIPS)),
            dma((links,)), dma((CHIPS,)), dma((CHIPS,)), dma((CHIPS,)),
        ],
        compiler_params=pltpu.CompilerParams(
            collective_id=0, has_side_effects=True, vmem_limit_bytes=56 * 2**20
        ),
        name="activity",
    )(expression, prior_values, support, gram)


def on_device(expression, prior_values, block_mask, gram_inverse):
    cell_devices = lax.axis_size("cell")
    cell_rows, gene_rows = expression.shape
    tf_total = prior_values.shape[1]
    gene_blocks, tf_blocks = block_mask.shape
    blocks = activity_of(expression, prior_values, block_mask, gram_inverse)
    activity_part = lax.dynamic_index_in_dim(blocks, lax.axis_index("gene"), 0, keepdims=False)
    activity_t = blocks.reshape(tf_total, cell_rows)
    widened = activity_t.astype(jnp.float32)
    sum_squares = lax.psum(jnp.sum(widened * widened), "cell")
    total_cells = cell_rows * cell_devices
    step_size = 0.5 / (sum_squares / (total_cells * tf_total) + EPSILON)
    tf_rows = tf_total // cell_devices
    first_row = lax.axis_index("cell") * tf_rows
    relief = block_mask.T.astype(jnp.float32)[:, None, :, None]
    penalty = jnp.broadcast_to(1.0 - PRIOR_RELIEF * relief, (tf_blocks, BLOCK, gene_blocks, BLOCK))
    penalty = lax.dynamic_slice_in_dim(penalty.reshape(tf_total, gene_rows), first_row, tf_rows, 0)
    limit = step_size * LASSO * penalty

    gram_part = lax.dot_general(
        activity_t,
        activity_part,
        (((1,), (1,)), ((), ())),
        preferred_element_type=jnp.float32,
    ).astype(jnp.bfloat16)
    first_term = jnp.dot(activity_t, expression, preferred_element_type=jnp.float32)
    first = lax.psum_scatter(
        first_term.astype(jnp.bfloat16), "cell", scatter_dimension=0, tiled=True
    ).astype(jnp.float32)
    gram_rows = lax.all_gather(
        lax.psum_scatter(gram_part, "cell", scatter_dimension=0, tiled=True),
        "gene",
        axis=1,
        tiled=True,
    )
    scale = step_size / total_cells
    coefficient = shrink(scale * first, limit, step_size)
    whole = lax.all_gather(coefficient.astype(jnp.bfloat16), "cell", axis=0, tiled=True)
    second = jnp.dot(gram_rows, whole, preferred_element_type=jnp.float32)
    coefficient = shrink(coefficient - scale * (second - first), limit, step_size)
    return coefficient * OUT_UNITS


def solution(mesh):
    in_specs = (P("cell", "gene"), P("gene", None), P("gene", None), P(None, "gene"))
    out_specs = P("cell", "gene")
    return jax.shard_map(
        on_device, mesh=mesh, in_specs=in_specs, out_specs=out_specs, check_vma=False
    )
```

```python
import functools

import jax
import jax.numpy as jnp
from jax import lax
from jax.experimental import pallas as pl
from jax.experimental.pallas import tpu as pltpu
from jax.sharding import PartitionSpec as P

BLOCK = 128

OUT_UNITS = 100.0
LASSO = 0.006
RIDGE = 0.1
PRIOR_RELIEF = 0.7
EPSILON = 1e-06

MESH = pl.DeviceIdType.MESH
CHIPS = 8
CHUNK = 256
OFFSETS = ((0, 1), (0, 3), (1, 0), (0, 2), (1, 1), (1, 3), (1, 2))


def activity_kernel(
    x_hbm, prior_hbm, support_ref, gram_ref, at_ref,
    x, prior, part, pair, total, got, scores, acc,
    x_sem, prior_sem, pair_send, pair_recv, rs_send, rs_recv,
    ag_send, ag_recv, fw_send, fw_recv, at_send, at_recv, af_send, af_recv,
):
    chunks = prior.shape[0]
    me = lax.axis_index("gene")
    core = me % 2
    chip = me // 2
    y, z = chip % 4, chip // 4
    partner = chip * 2 + (1 - core)
    others = [((z + dz) % 2) * 4 + (y + dy) % 4 for dz, dy in OFFSETS]

    x_copy = pltpu.make_async_copy(x_hbm, x, x_sem)
    x_copy.start()

    def prior_copy(n):
        columns = pl.ds(pl.multiple_of(n * CHUNK, CHUNK), CHUNK)
        return pltpu.make_async_copy(prior_hbm.at[:, columns], prior.at[n], prior_sem.at[n])

    for n in range(chunks):
        prior_copy(n).start()

    barrier = pltpu.get_barrier_semaphore()
    for device in [other * 2 + core for other in others] + [partner]:
        pl.semaphore_signal(barrier, inc=1, device_id={"gene": device}, device_id_type=MESH)
    pl.semaphore_wait(barrier, len(others) + 1)

    def remote(src, dst, send, recv, device):
        return pltpu.make_async_remote_copy(
            src_ref=src, dst_ref=dst, send_sem=send, recv_sem=recv,
            device_id={"gene": device}, device_id_type=MESH,
        )

    def pair_copy(n):
        return remote(
            part.at[n, :, 1 - core], pair.at[n], pair_send.at[n], pair_recv.at[n], partner
        )

    def rs_copy(n, o, slot):
        return remote(
            total.at[n, others[o]], got.at[n, slot], rs_send.at[n, o], rs_recv.at[n, slot],
            others[o] * 2 + core,
        )

    def ag_copy(n, o, slot):
        block = scores.at[n, slot, core]
        return remote(block, block, ag_send.at[n, o], ag_recv.at[n, slot], others[o] * 2 + core)

    def fw_copy(n, slot, side):
        block = scores.at[n, slot, side]
        return remote(block, block, fw_send.at[n, slot], fw_recv.at[n, slot], partner)

    def at_copy(o, slot):
        block = at_ref.at[slot * 2 + core]
        return remote(block, block, at_send.at[o], at_recv.at[slot], others[o] * 2 + core)

    def af_copy(slot, side):
        block = at_ref.at[slot * 2 + side]
        return remote(block, block, af_send.at[slot], af_recv.at[slot], partner)

    x_copy.wait()

    def spread(n):
        pair_copy(n).wait_recv()
        own = part[n, :, core].astype(jnp.float32)
        total[n] = (own + pair[n].astype(jnp.float32)).astype(jnp.bfloat16)
        for o in range(len(others)):
            rs_copy(n, o, chip).start()

    def multiply(n, carry):
        prior_copy(n).wait()
        masked = prior[n].reshape(-1, BLOCK // 16, 16, CHUNK) * support_ref[n][:, None]
        prior[n] = masked.reshape(prior.shape[1:])
        product = jnp.dot(x[...], prior[n], preferred_element_type=jnp.float32)
        part[n] = product.astype(jnp.bfloat16).reshape(part.shape[1:])
        pair_copy(n).start()

        @pl.when(n > 0)
        def _():
            spread(n - 1)

        return carry

    lax.fori_loop(0, chunks, multiply, 0)
    spread(chunks - 1)

    def collect(n, carry):
        value = total[n, chip].astype(jnp.float32)
        for o in range(len(others)):
            rs_copy(n, o, others[o]).wait_recv()
            value = value + got[n, others[o]].astype(jnp.float32)
        scores[n, chip, core] = value.astype(jnp.bfloat16)
        for o in range(len(others)):
            ag_copy(n, o, chip).start()
        fw_copy(n, chip, core).start()
        return carry

    lax.fori_loop(0, chunks, collect, 0)

    def forward(n, carry):
        for o in range(len(others)):
            ag_copy(n, o, others[o]).wait_recv()
            fw_copy(n, others[o], core).start()
        return carry

    lax.fori_loop(0, chunks, forward, 0)

    acc[...] = jnp.zeros_like(acc)

    def mix(n, carry):
        for slot in range(CHIPS):
            fw_copy(n, slot, 1 - core).wait_recv()
        acc[...] += lax.dot_general(
            gram_ref[n], scores[n].reshape(-1, CHUNK), (((1,), (1,)), ((), ())),
            preferred_element_type=jnp.float32,
        )
        return carry

    lax.fori_loop(0, chunks, mix, 0)
    at_ref[me] = acc[...].astype(jnp.bfloat16)
    for o in range(len(others)):
        at_copy(o, chip).start()
    af_copy(chip, core).start()
    for o in range(len(others)):
        at_copy(o, others[o]).wait_recv()
        af_copy(others[o], core).start()
    for slot in range(CHIPS):
        af_copy(slot, 1 - core).wait_recv()

    def drain(n, carry):
        pair_copy(n).wait_send()
        for o in range(len(others)):
            rs_copy(n, o, chip).wait_send()
            ag_copy(n, o, chip).wait_send()
        for slot in range(CHIPS):
            fw_copy(n, slot, core).wait_send()
        return carry

    lax.fori_loop(0, chunks, drain, 0)
    for o in range(len(others)):
        at_copy(o, chip).wait_send()
    for slot in range(CHIPS):
        af_copy(slot, core).wait_send()


def activity_of(expression, prior_values, block_mask, gram_inverse):
    devices = lax.axis_size("gene")
    cells, genes = expression.shape
    factors = prior_values.shape[1]
    own = gram_inverse.shape[1]
    chunks = factors // CHUNK
    rows = cells // devices
    support = jnp.repeat(block_mask.astype(jnp.bfloat16), BLOCK, axis=1)
    support = support.reshape(genes // BLOCK, chunks, 1, CHUNK).transpose(1, 0, 2, 3)
    support = jnp.broadcast_to(support, (chunks, genes // BLOCK, 16, CHUNK))
    gram = gram_inverse.T.reshape(own, chunks, CHUNK).transpose(1, 0, 2)
    bf = jnp.bfloat16
    dma = pltpu.SemaphoreType.DMA
    links = len(OFFSETS)
    return pl.pallas_call(
        activity_kernel,
        out_shape=jax.ShapeDtypeStruct((devices, own, cells), bf),
        in_specs=[pl.BlockSpec(memory_space=pl.ANY)] * 2
        + [pl.BlockSpec(memory_space=pltpu.VMEM)] * 2,
        out_specs=pl.BlockSpec(memory_space=pltpu.VMEM),
        scratch_shapes=[
            pltpu.VMEM((cells, genes), bf),
            pltpu.VMEM((chunks, genes, CHUNK), bf),
            pltpu.VMEM((chunks, CHIPS, 2, rows, CHUNK), bf),
            pltpu.VMEM((chunks, CHIPS, rows, CHUNK), bf),
            pltpu.VMEM((chunks, CHIPS, rows, CHUNK), bf),
            pltpu.VMEM((chunks, CHIPS, rows, CHUNK), bf),
            pltpu.VMEM((chunks, CHIPS, 2, rows, CHUNK), bf),
            pltpu.VMEM((own, cells), jnp.float32),
            dma, dma((chunks,)), dma((chunks,)), dma((chunks,)),
            dma((chunks, links)), dma((chunks, CHIPS)),
            dma((chunks, links)), dma((chunks, CHIPS)),
            dma((chunks, CHIPS)), dma((chunks, CHIPS)),
            dma((links,)), dma((CHIPS,)), dma((CHIPS,)), dma((CHIPS,)),
        ],
        compiler_params=pltpu.CompilerParams(
            collective_id=0, has_side_effects=True, vmem_limit_bytes=56 * 2**20
        ),
        name="activity",
    )(expression, prior_values, support, gram)


Z_ROWS = 1024
HOPS = 4


def solve_kernel(
    at_ref, x_hbm, relief_ref, out_ref,
    x, part, z1, zs, x1, x2, xs, z2, gram_part, gram_got, gram, squares, penalty,
    first, coef, coef_bf, sent,
    x_sem, z1_send, z1_recv, x1_send, x1_recv, x2_send, x2_recv, z2_send, z2_recv,
    gp_send, gp_recv, gc_send, gc_recv, gg_send, gg_recv, gf_send, gf_recv,
    sq_send, sq_recv, out_send, out_recv,
):
    cells = 2 * HOPS
    pieces = gram_part.shape[0]
    factors, width = first.shape
    cell, gene = lax.axis_index("cell"), lax.axis_index("gene")
    x_at, z_lo = cell % HOPS, cell // HOPS
    core, y_at, z_hi = gene % 2, (gene // 2) % 4, gene // 8
    z_partner = (1 - z_lo) * HOPS + x_at
    core_partner = z_hi * 8 + y_at * 2 + (1 - core)
    near = [(cell, z_hi * 8 + ((y_at + dy) % 4) * 2 + core) for dy in (1, 3, 2)]
    near += [(z_partner, (1 - z_hi) * 8 + ((y_at + dy) % 4) * 2 + core) for dy in (0, 1, 3, 2)]

    def remote(src, dst, send, recv, at_cell, at_gene):
        return pltpu.make_async_remote_copy(
            src_ref=src, dst_ref=dst, send_sem=send, recv_sem=recv,
            device_id={"cell": at_cell, "gene": at_gene}, device_id_type=MESH,
        )

    tail = x_hbm.shape[1] - (cells - 1) * width

    def x_copy(d):
        lanes = tail if d == cells - 1 else width
        return pltpu.make_async_copy(
            x_hbm.at[:, pl.ds(d * width, lanes)], x.at[d, :, pl.ds(0, lanes)], x_sem.at[d]
        )

    for d in range(cells):
        x_copy(d).start()
    x[cells - 1, :, tail:] = jnp.zeros((x.shape[1], width - tail), x.dtype)

    barrier = pltpu.get_barrier_semaphore()
    greeted = [((cell + o) % cells, gene) for o in range(1, cells)]
    greeted += near + [(cell, core_partner)]
    for at_cell, at_gene in greeted:
        pl.semaphore_signal(
            barrier, inc=1, device_id={"cell": at_cell, "gene": at_gene}, device_id_type=MESH
        )
    pl.semaphore_wait(barrier, len(greeted))

    whole = at_ref[...].reshape(factors, -1)
    product = lax.dot_general(
        at_ref[gene], whole, (((1,), (1,)), ((), ())), preferred_element_type=jnp.float32
    )
    gram_part[...] = product.astype(jnp.bfloat16).reshape(gram_part.shape)

    def gp_copy(r, slot):
        return remote(gram_part.at[r], gram_got.at[slot], gp_send.at[r], gp_recv.at[slot], r, gene)

    for r in range(pieces):
        @pl.when(cell != r)
        def _():
            gp_copy(r, cell).start()

    for d in range(cells):
        x_copy(d).wait()

    def z1_copy(x_to):
        d = (1 - z_lo) * HOPS + x_to
        return remote(
            part.at[d, pl.ds(0, Z_ROWS)], z1.at[x_to], z1_send.at[x_to], z1_recv.at[x_to],
            z_partner, gene,
        )

    rest = pl.ds(Z_ROWS, factors - Z_ROWS)

    def x1_copy(z_to, x_to, slot):
        return remote(
            part.at[z_to * HOPS + x_to, rest], x1.at[slot, z_to],
            x1_send.at[x_to, z_to], x1_recv.at[slot, z_to], z_lo * HOPS + x_to, gene,
        )

    def x2_copy(x_to, slot):
        return remote(
            zs.at[x_to], x2.at[slot], x2_send.at[x_to], x2_recv.at[slot],
            z_lo * HOPS + x_to, gene,
        )

    def z2_copy():
        return remote(xs, z2, z2_send, z2_recv, z_partner, gene)

    def multiply(i, carry):
        x_to = (x_at + 1 + i) % HOPS
        z_to = (z_lo + 1 + i // HOPS) % 2
        d = z_to * HOPS + x_to
        value = jnp.dot(
            at_ref[...].reshape(factors, -1), x[d], preferred_element_type=jnp.float32
        )
        part[d] = value.astype(jnp.bfloat16)

        @pl.when(i < HOPS)
        def _():
            z1_copy(x_to).start()

        @pl.when(x_to != x_at)
        def _():
            x1_copy(z_to, x_to, x_at).start()

        return carry

    lax.fori_loop(0, cells, multiply, 0)

    def gc_copy(t, r):
        block = gram.at[gene, r]
        return remote(block, block, gc_send.at[t], gc_recv.at[r], t, gene)

    for r in range(pieces):
        @pl.when(cell == r)
        def _():
            value = gram_part[r].astype(jnp.float32)
            for o in range(1, cells):
                slot = (cell + o) % cells
                gp_copy(r, slot).wait_recv()
                value = value + gram_got[slot].astype(jnp.float32)
            gram[gene, r] = value.astype(jnp.bfloat16)
            for o in range(1, cells):
                gc_copy((cell + o) % cells, r).start()

    def sq_copy(t, slot):
        return remote(squares.at[slot], squares.at[slot], sq_send.at[t], sq_recv.at[slot], t, gene)

    def square(b, total):
        value = at_ref[b].astype(jnp.float32)
        return total + jnp.sum((value * value).reshape(-1, 8, value.shape[1]), axis=0)

    squares[cell] = lax.fori_loop(
        0, at_ref.shape[0], square, jnp.zeros(squares.shape[1:], jnp.float32)
    )
    for o in range(1, cells):
        sq_copy((cell + o) % cells, cell).start()

    for b in range(relief_ref.shape[0]):
        rows = jnp.broadcast_to(relief_ref[b][None], (BLOCK // 8, 8, width))
        penalty[pl.ds(b * BLOCK, BLOCK)] = rows.reshape(BLOCK, width)

    def pair_sum(i):
        x_to = (x_at + 1 + i) % HOPS
        z1_copy(x_to).wait_recv()
        own = part[z_lo * HOPS + x_to, :Z_ROWS].astype(jnp.float32)
        zs[x_to] = (own + z1[x_to].astype(jnp.float32)).astype(jnp.bfloat16)
        if i < HOPS - 1:
            x2_copy(x_to, x_at).start()

    pair_sum(0)

    def gg_copy(k, slot):
        at_cell, at_gene = near[k]
        return remote(
            gram.at[slot], gram.at[slot], gg_send.at[k], gg_recv.at[slot], at_cell, at_gene
        )

    def gf_copy(slot):
        return remote(
            gram.at[slot], gram.at[slot], gf_send.at[slot // 2], gf_recv.at[slot], cell, core_partner
        )

    for r in range(pieces):
        @pl.when(cell != r)
        def _():
            gc_copy(cell, r).wait_recv()

    for k in range(len(near)):
        gg_copy(k, gene).start()
    gf_copy(gene).start()

    def forward(k):
        slot = near[k][1]
        gg_copy(k, slot).wait_recv()
        gf_copy(slot).start()

    pair_sum(1)
    pair_sum(2)

    value = part[(1 - z_lo) * HOPS + x_at, Z_ROWS:].astype(jnp.float32)
    for o in range(1, HOPS):
        slot = (x_at + o) % HOPS
        x1_copy(1 - z_lo, x_at, slot).wait_recv()
        value = value + x1[slot, 1 - z_lo].astype(jnp.float32)
    xs[...] = value.astype(jnp.bfloat16)
    z2_copy().start()

    pair_sum(3)

    for k in range(len(near)):
        forward(k)

    for o in range(1, cells):
        sq_copy(cell, (cell + o) % cells).wait_recv()
    sum_squares = jnp.sum(jnp.sum(squares[...], axis=0), keepdims=True)
    total_cells = cells * x.shape[1]
    step_size = 0.5 / (sum_squares / (total_cells * factors) + EPSILON)
    scale = step_size / total_cells
    inverse = 1.0 / (1.0 + step_size * RIDGE)

    def shrunk(moved, rows):
        limit = step_size * penalty[rows]
        return (jnp.maximum(moved - limit, 0.0) - jnp.maximum(-moved - limit, 0.0)) * inverse

    def start_from(value, rows):
        first[rows] = value
        start = shrunk(scale * value, rows)
        coef[rows] = start
        coef_bf[rows] = start.astype(jnp.bfloat16)

    for o in range(1, HOPS):
        slot = (x_at + o) % HOPS
        x2_copy(x_at, slot).wait_recv()
        x1_copy(z_lo, x_at, slot).wait_recv()

    def z_block(b, carry):
        rows = pl.ds(pl.multiple_of(b * BLOCK, BLOCK), BLOCK)
        value = zs[x_at, rows].astype(jnp.float32)
        for o in range(1, HOPS):
            value = value + x2[(x_at + o) % HOPS, rows].astype(jnp.float32)
        start_from(value, rows)
        return carry

    lax.fori_loop(0, Z_ROWS // BLOCK, z_block, 0)
    z2_copy().wait_recv()

    def x_block(b, carry):
        low = pl.ds(pl.multiple_of(b * BLOCK, BLOCK), BLOCK)
        rows = pl.ds(pl.multiple_of(b * BLOCK + Z_ROWS, BLOCK), BLOCK)
        value = part[cell, rows].astype(jnp.float32) + z2[low].astype(jnp.float32)
        for o in range(1, HOPS):
            value = value + x1[(x_at + o) % HOPS, z_lo, low].astype(jnp.float32)
        start_from(value, rows)
        return carry

    lax.fori_loop(0, (factors - Z_ROWS) // BLOCK, x_block, 0)

    gf_slots = [n * 2 + 1 - core for n in range(gram.shape[0] // 2)]
    for slot in gf_slots:
        gf_copy(slot).wait_recv()

    height = out_ref.shape[1]

    def out_copy(t, slot):
        return remote(sent.at[t], out_ref.at[slot], out_send.at[t], out_recv.at[slot], t, gene)

    def finish(i, carry):
        t = (cell + 1 + i) % cells
        rows = pl.ds(pl.multiple_of(t * height, 32), height)
        block = gram[pl.ds(t * 2, 2)].reshape(height, factors)
        second = jnp.dot(block, coef_bf[...], preferred_element_type=jnp.float32)
        moved = coef[rows] - scale * (second - first[rows])
        value = (shrunk(moved, rows) * OUT_UNITS).astype(jnp.bfloat16)

        @pl.when(i < cells - 1)
        def _():
            sent[t] = value
            out_copy(t, cell).start()

        @pl.when(i == cells - 1)
        def _():
            out_ref[cell] = value

        return carry

    lax.fori_loop(0, cells, finish, 0)

    for r in range(pieces):
        @pl.when(cell != r)
        def _():
            gp_copy(r, cell).wait_send()

        @pl.when(cell == r)
        def _():
            for o in range(1, cells):
                gc_copy((cell + o) % cells, r).wait_send()

    for x_to in range(HOPS):
        z1_copy(x_to).wait_send()
    for o in range(1, HOPS):
        x_to = (x_at + o) % HOPS
        x2_copy(x_to, x_at).wait_send()
        for z_to in range(2):
            x1_copy(z_to, x_to, x_at).wait_send()
    z2_copy().wait_send()
    for k in range(len(near)):
        gg_copy(k, gene).wait_send()
    for n in range(gram.shape[0] // 2):
        gf_copy(n * 2 + core).wait_send()
    for o in range(1, cells):
        t = (cell + o) % cells
        sq_copy(t, cell).wait_send()
        out_copy(t, cell).wait_send()
        out_copy(cell, t).wait_recv()


def solve(activity_t, expression, block_mask):
    cell_devices, gene_devices = lax.axis_size("cell"), lax.axis_size("gene")
    _, own, cells = activity_t.shape
    factors = gene_devices * own
    width = CHUNK
    gene_blocks, tf_blocks = block_mask.shape
    per = width // BLOCK
    relief = jnp.pad(block_mask.T.astype(jnp.float32), ((0, 0), (0, cell_devices * per - gene_blocks)))
    relief = lax.dynamic_slice_in_dim(relief, lax.axis_index("cell") * per, per, 1)
    relief = jnp.repeat(LASSO * (1.0 - PRIOR_RELIEF * relief), BLOCK, axis=1)
    relief = jnp.broadcast_to(relief[:, None], (tf_blocks, 8, width))
    pieces = own // 16
    rest = factors - Z_ROWS
    bf, f32 = jnp.bfloat16, jnp.float32
    vmem, dma = pltpu.VMEM, pltpu.SemaphoreType.DMA
    return pl.pallas_call(
        solve_kernel,
        out_shape=jax.ShapeDtypeStruct((cell_devices, factors // cell_devices, width), bf),
        in_specs=[
            pl.BlockSpec(memory_space=pltpu.VMEM),
            pl.BlockSpec(memory_space=pl.ANY),
            pl.BlockSpec(memory_space=pltpu.VMEM),
        ],
        out_specs=pl.BlockSpec(memory_space=pltpu.VMEM),
        scratch_shapes=[
            vmem((cell_devices, cells, width), bf),
            vmem((cell_devices, factors, width), bf),
            vmem((HOPS, Z_ROWS, width), bf),
            vmem((HOPS, Z_ROWS, width), bf),
            vmem((HOPS, 2, rest, width), bf),
            vmem((HOPS, Z_ROWS, width), bf),
            vmem((rest, width), bf),
            vmem((rest, width), bf),
            vmem((pieces, 16, factors), bf),
            vmem((cell_devices, 16, factors), bf),
            vmem((gene_devices, pieces, 16, factors), bf),
            vmem((cell_devices, 8, cells), f32),
            vmem((factors, width), f32),
            vmem((factors, width), f32),
            vmem((factors, width), f32),
            vmem((factors, width), bf),
            vmem((cell_devices, factors // cell_devices, width), bf),
            dma((cell_devices,)),
            dma((HOPS,)), dma((HOPS,)),
            dma((HOPS, 2)), dma((HOPS, 2)),
            dma((HOPS,)), dma((HOPS,)),
            dma, dma,
            dma((pieces,)), dma((cell_devices,)),
            dma((cell_devices,)), dma((pieces,)),
            dma((7,)), dma((gene_devices,)),
            dma((gene_devices // 2,)), dma((gene_devices,)),
            dma((cell_devices,)), dma((cell_devices,)),
            dma((cell_devices,)), dma((cell_devices,)),
        ],
        compiler_params=pltpu.CompilerParams(
            collective_id=1, has_side_effects=True, vmem_limit_bytes=60 * 2**20
        ),
        name="solve",
    )(activity_t, expression, relief)


def on_device(expression, prior_values, block_mask, gram_inverse):
    activity_t = activity_of(expression, prior_values, block_mask, gram_inverse)
    blocks = solve(activity_t, expression, block_mask)
    rows = blocks.shape[1]
    whole = blocks.transpose(1, 0, 2).reshape(rows, -1)
    return whole[:, : expression.shape[1]].astype(jnp.float32)


def solution(mesh):
    in_specs = (P("cell", "gene"), P("gene", None), P("gene", None), P(None, "gene"))
    out_specs = P("cell", "gene")
    return jax.shard_map(
        on_device, mesh=mesh, in_specs=in_specs, out_specs=out_specs, check_vma=False
    )
```

```python
import functools

import jax
import jax.numpy as jnp
from jax import lax
from jax.experimental import pallas as pl
from jax.experimental.pallas import tpu as pltpu
from jax.sharding import PartitionSpec as P

BLOCK = 128

OUT_UNITS = 100.0
LASSO = 0.006
RIDGE = 0.1
PRIOR_RELIEF = 0.7
EPSILON = 1e-06

MESH = pl.DeviceIdType.MESH
CHUNK = 256
SPLIT = 48
LAGS = (0, 1, 3, 5, 7, 9, 10)


class Spread:
    def __init__(self, ref, at, low, high, ys, across, partner, direct, handed):
        self.ref, (self.z, self.y, self.core) = ref, at
        self.rows = (low, high)
        self.ys, self.across, self.partner = ys, across, partner
        self.y_send, self.y_recv, self.z_send, self.z_recv, self.own_send, self.own_recv = direct
        self.fy_send, self.fy_recv, self.fz_send, self.fz_recv = handed

    def remote(self, block, send, recv, device):
        return pltpu.make_async_remote_copy(
            src_ref=block, dst_ref=block, send_sem=send, recv_sem=recv,
            device_id=device, device_id_type=MESH,
        )

    def own(self, side):
        block = self.ref.at[self.z, self.y, side]
        return self.remote(block, self.own_send, self.own_recv, self.partner)

    def over_y(self, k, device, y_to, slot):
        zs = slice(None) if k else self.z
        block = self.ref.at[zs, slot, self.core, self.rows[k]]
        return self.remote(block, self.y_send.at[k, y_to], self.y_recv.at[k, slot], device)

    def over_z(self, k, side):
        ys = self.y if k else slice(None)
        block = self.ref.at[side, ys, self.core, self.rows[k]]
        return self.remote(block, self.z_send.at[k], self.z_recv.at[k], self.across)

    def hand_y(self, k, slot, side):
        zs = slice(None) if k else self.z
        block = self.ref.at[zs, slot, side, self.rows[k]]
        return self.remote(block, self.fy_send.at[k, slot], self.fy_recv.at[k, slot], self.partner)

    def hand_z(self, k, side):
        ys = self.y if k else slice(None)
        block = self.ref.at[1 - self.z, ys, side, self.rows[k]]
        return self.remote(block, self.fz_send.at[k], self.fz_recv.at[k], self.partner)

    def begin(self):
        self.over_z(1, self.z).start()
        for y_to, device in self.ys:
            self.over_y(0, device, y_to, self.y).start()
        self.own(self.core).start()

    def relay_high(self):
        self.over_z(1, 1 - self.z).wait_recv()
        for y_to, device in self.ys:
            self.over_y(1, device, y_to, self.y).start()
        self.hand_z(1, self.core).start()

    def relay_low(self):
        for slot, device in self.ys:
            self.over_y(0, device, self.y, slot).wait_recv()
        self.over_z(0, self.z).start()
        for slot, _ in self.ys:
            self.hand_y(0, slot, self.core).start()

    def finish(self):
        for slot, device in self.ys:
            self.over_y(1, device, self.y, slot).wait_recv()
            self.hand_y(1, slot, self.core).start()
        self.over_z(0, 1 - self.z).wait_recv()
        self.hand_z(0, self.core).start()
        self.own(1 - self.core).wait_recv()
        for k in range(2):
            self.hand_z(k, 1 - self.core).wait_recv()
            for slot, _ in self.ys:
                self.hand_y(k, slot, 1 - self.core).wait_recv()

    def drain(self):
        self.own(self.core).wait_send()
        for k in range(2):
            self.over_z(k, self.z).wait_send()
            self.hand_z(k, self.core).wait_send()
            for y_to, device in self.ys:
                self.over_y(k, device, y_to, self.y).wait_send()
                self.hand_y(k, y_to, self.core).wait_send()


def activity_kernel(
    x_hbm, prior_hbm, mask_ref, gram_ref, at_ref,
    x, prior, support, part, pair, total, near_z, near_y, mid_z, mid_y, last_z, last_y, scores, acc,
    x_sem, prior_sem, pair_send, pair_recv,
    rs_y_send, rs_y_recv, rs_z_send, rs_z_recv,
    ag_y_send, ag_y_recv, ag_z_send, ag_z_recv, fw_send, fw_recv,
    at_y_send, at_y_recv, at_z_send, at_z_recv, own_send, own_recv,
    af_y_send, af_y_recv, af_z_send, af_z_recv,
):
    chunks, genes, _ = prior.shape
    me = lax.axis_index("gene")
    core, y, z = me % 2, (me // 2) % 4, me // 8
    partner = z * 8 + y * 2 + (1 - core)
    across = (1 - z) * 8 + y * 2 + core
    turns = (1, 3, 2)
    ys = [(y + dy) % 4 for dy in turns]

    x_copy = pltpu.make_async_copy(x_hbm, x, x_sem)

    def prior_copy(n):
        columns = pl.ds(pl.multiple_of(n * CHUNK, CHUNK), CHUNK)
        return pltpu.make_async_copy(prior_hbm.at[:, columns], prior.at[n], prior_sem.at[n])

    prior_copy(0).start()
    x_copy.start()
    for n in range(1, chunks):
        prior_copy(n).start()

    def device_of(y_to):
        return z * 8 + y_to * 2 + core

    barrier = pltpu.get_barrier_semaphore()
    for device in [device_of(y_to) for y_to in ys] + [across, partner]:
        pl.semaphore_signal(barrier, inc=1, device_id={"gene": device}, device_id_type=MESH)
    pl.semaphore_wait(barrier, len(ys) + 2)

    for b in range(mask_ref.shape[1]):
        lanes = slice(b % 2 * BLOCK, b % 2 * BLOCK + BLOCK)
        support[b // 2, :, lanes] = jnp.broadcast_to(
            mask_ref[:, b : b + 1].astype(jnp.float32), (support.shape[1], BLOCK)
        )

    def remote(src, dst, send, recv, device):
        return pltpu.make_async_remote_copy(
            src_ref=src, dst_ref=dst, send_sem=send, recv_sem=recv,
            device_id={"gene": device}, device_id_type=MESH,
        )

    def pair_copy(n):
        return remote(
            part.at[n, :, :, 1 - core], pair.at[n], pair_send.at[n], pair_recv.at[n], partner
        )

    def rs_y(n, z_first, y_to, slot):
        if z_first:
            src, dst = mid_z.at[n, y_to], last_z.at[n, slot]
        else:
            src, dst = total.at[n, :, y_to], near_y.at[n, slot]
        return remote(src, dst, rs_y_send.at[n, y_to], rs_y_recv.at[n, slot], device_of(y_to))

    def rs_z(n, z_first):
        if z_first:
            src, dst = total.at[n, 1 - z], near_z.at[n]
        else:
            src, dst = mid_y.at[n, 1 - z], last_y.at[n]
        return remote(src, dst, rs_z_send.at[n], rs_z_recv.at[n], across)

    def ag_y(n, z_first, y_to, slot):
        block = scores.at[n, :, slot, core] if z_first else scores.at[n, z, slot, core]
        return remote(
            block, block, ag_y_send.at[n, y_to], ag_y_recv.at[n, slot], device_of(y_to)
        )

    def ag_z(n, z_first, side):
        block = scores.at[n, side, y, core] if z_first else scores.at[n, side, :, core]
        return remote(block, block, ag_z_send.at[n], ag_z_recv.at[n], across)

    def fw_copy(n, side):
        block = scores.at[n, :, :, side]
        return remote(block, block, fw_send.at[n], fw_recv.at[n], partner)

    def wide(value):
        return value.astype(jnp.float32)

    def by_order(n, parity, step):
        @pl.when(n % 2 == parity)
        def _():
            step(True)

        @pl.when(n % 2 != parity)
        def _():
            step(False)

    def multiply(n):
        prior_copy(n).wait()

        rows = jnp.broadcast_to(support[n][:, None], (support.shape[1], 16, CHUNK))
        masked = prior[n].reshape(-1, BLOCK // 16, 16, CHUNK) * rows.astype(jnp.bfloat16)[:, None]
        prior[n] = masked.reshape(prior.shape[1:])
        product = jnp.dot(x[...], prior[n], preferred_element_type=jnp.float32)
        part[n] = product.astype(jnp.bfloat16).reshape(part.shape[1:])
        pair_copy(n).start()

    def spread(n):
        pair_copy(n).wait_recv()
        total[n] = (wide(part[n, :, :, core]) + wide(pair[n])).astype(jnp.bfloat16)

        def step(z_first):
            if z_first:
                rs_z(n, True).start()
            else:
                for y_to in ys:
                    rs_y(n, False, y_to, y).start()

        by_order(n, 0, step)

    def middle(n):
        def step(z_first):
            if z_first:
                rs_z(n, True).wait_recv()
                mid_z[n] = (wide(total[n, z]) + wide(near_z[n])).astype(jnp.bfloat16)
                for y_to in ys:
                    rs_y(n, True, y_to, y).start()
            else:
                value = wide(total[n, :, y])
                for slot in ys:
                    rs_y(n, False, y, slot).wait_recv()
                    value = value + wide(near_y[n, slot])
                mid_y[n] = value.astype(jnp.bfloat16)
                rs_z(n, False).start()

        by_order(n, 0, step)

    def collect(n):
        def step(z_first):
            if z_first:
                value = wide(mid_z[n, y])
                for slot in ys:
                    rs_y(n, True, y, slot).wait_recv()
                    value = value + wide(last_z[n, slot])
            else:
                rs_z(n, False).wait_recv()
                value = wide(mid_y[n, z]) + wide(last_y[n])
            scores[n, z, y, core] = value.astype(jnp.bfloat16)

        by_order(n, 0, step)

        def out(z_first):
            if z_first:
                ag_z(n, True, z).start()
            else:
                for y_to in ys:
                    ag_y(n, False, y_to, y).start()

        by_order(n, 1, out)

    def relay(n):
        def step(z_first):
            if z_first:
                ag_z(n, True, 1 - z).wait_recv()
                for y_to in ys:
                    ag_y(n, True, y_to, y).start()
            else:
                for slot in ys:
                    ag_y(n, False, y, slot).wait_recv()
                ag_z(n, False, z).start()

        by_order(n, 1, step)

    def share(n):
        def step(z_first):
            if z_first:
                for slot in ys:
                    ag_y(n, True, y, slot).wait_recv()
            else:
                ag_z(n, False, 1 - z).wait_recv()

        by_order(n, 1, step)
        fw_copy(n, core).start()

    acc[...] = jnp.zeros_like(acc)

    def mix(n):
        fw_copy(n, 1 - core).wait_recv()
        lanes = pl.ds(pl.multiple_of(n * CHUNK, CHUNK), CHUNK)
        acc[...] += lax.dot_general(
            gram_ref[:, lanes], scores[n].reshape(-1, CHUNK), (((1,), (1,)), ((), ())),
            preferred_element_type=jnp.float32,
        )

    x_copy.wait()
    stages = (
        (LAGS[0], multiply), (LAGS[1], spread), (LAGS[2], middle), (LAGS[3], collect),
        (LAGS[4], relay), (LAGS[5], share), (LAGS[6], mix),
    )

    def turn(i, carry):
        for lag, stage in stages:
            @pl.when((i >= lag) & (i < lag + chunks))
            def _():
                stage(i - lag)

        return carry

    lax.fori_loop(0, chunks + LAGS[-1], turn, 0)

    at_ref[z, y, core] = acc[...].astype(jnp.bfloat16)
    spread_at = Spread(
        at_ref, (z, y, core), slice(0, SPLIT), slice(SPLIT, at_ref.shape[3]),
        [(y_to, {"gene": device_of(y_to)}) for y_to in ys], {"gene": across}, {"gene": partner},
        (at_y_send, at_y_recv, at_z_send, at_z_recv, own_send, own_recv),
        (af_y_send, af_y_recv, af_z_send, af_z_recv),
    )
    spread_at.begin()
    spread_at.relay_high()
    spread_at.relay_low()
    spread_at.finish()

    def drain(n, carry):
        pair_copy(n).wait_send()
        fw_copy(n, core).wait_send()

        def reduced(z_first):
            rs_z(n, z_first).wait_send()
            for y_to in ys:
                rs_y(n, z_first, y_to, y).wait_send()

        by_order(n, 0, reduced)

        def gathered(z_first):
            ag_z(n, z_first, z).wait_send()
            for y_to in ys:
                ag_y(n, z_first, y_to, y).wait_send()

        by_order(n, 1, gathered)
        return carry

    lax.fori_loop(0, chunks, drain, 0)
    spread_at.drain()


def activity_of(expression, prior_values, block_mask, gram_inverse):
    devices = lax.axis_size("gene")
    cells, genes = expression.shape
    factors = prior_values.shape[1]
    own = gram_inverse.shape[1]
    chunks = factors // CHUNK
    rows = cells // devices
    bf = jnp.bfloat16
    vmem, dma = pltpu.VMEM, pltpu.SemaphoreType.DMA
    blocks = pl.pallas_call(
        activity_kernel,
        out_shape=jax.ShapeDtypeStruct((2, 4, 2, own, cells), bf),
        in_specs=[pl.BlockSpec(memory_space=pl.ANY)] * 2
        + [pl.BlockSpec(memory_space=pltpu.VMEM)] * 2,
        out_specs=pl.BlockSpec(memory_space=pltpu.VMEM),
        scratch_shapes=[
            vmem((cells, genes), bf),
            vmem((chunks, genes, CHUNK), bf),
            vmem((chunks, genes // BLOCK, CHUNK), jnp.float32),
            vmem((chunks, 2, 4, 2, rows, CHUNK), bf),
            vmem((chunks, 2, 4, rows, CHUNK), bf),
            vmem((chunks, 2, 4, rows, CHUNK), bf),
            vmem((chunks, 4, rows, CHUNK), bf),
            vmem((chunks, 4, 2, rows, CHUNK), bf),
            vmem((chunks, 4, rows, CHUNK), bf),
            vmem((chunks, 2, rows, CHUNK), bf),
            vmem((chunks, 4, rows, CHUNK), bf),
            vmem((chunks, rows, CHUNK), bf),
            vmem((chunks, 2, 4, 2, rows, CHUNK), bf),
            vmem((own, cells), jnp.float32),
            dma, dma((chunks,)), dma((chunks,)), dma((chunks,)),
            dma((chunks, 4)), dma((chunks, 4)), dma((chunks,)), dma((chunks,)),
            dma((chunks, 4)), dma((chunks, 4)), dma((chunks,)), dma((chunks,)),
            dma((chunks,)), dma((chunks,)),
            dma((2, 4)), dma((2, 4)), dma((2,)), dma((2,)), dma, dma,
            dma((2, 4)), dma((2, 4)), dma((2,)), dma((2,)),
        ],
        compiler_params=pltpu.CompilerParams(
            collective_id=0, has_side_effects=True, vmem_limit_bytes=56 * 2**20
        ),
        name="activity",
    )(expression, prior_values, block_mask, gram_inverse.T)
    return blocks


Z_ROWS = 1024
HOPS = 4
HELD = 5


def solve_kernel(
    at_ref, x_hbm, relief_ref, out_ref,
    x, part, z1, zs, x1, x2, xs, z2, gram_part, gram_z, gram_mid, gram_x, gram, squares, penalty,
    first, coef, coef_bf, sent,
    x_sem, z1_send, z1_recv, x1_send, x1_recv, x2_send, x2_recv, z2_send, z2_recv,
    gz_send, gz_recv, gx_send, gx_recv, hx_send, hx_recv, hz_send, hz_recv,
    gy_send, gy_recv, ga_send, ga_recv, own_send, own_recv, fy_send, fy_recv, fz_send, fz_recv,
    sq_send, sq_recv, out_send, out_recv,
):
    cells = 2 * HOPS
    pieces = at_ref.shape[3] // 16
    factors, width = first.shape
    cell, gene = lax.axis_index("cell"), lax.axis_index("gene")
    x_at, z_lo = cell % HOPS, cell // HOPS
    core, y_at, z_hi = gene % 2, (gene // 2) % 4, gene // 8
    z_partner = (1 - z_lo) * HOPS + x_at
    core_partner = z_hi * 8 + y_at * 2 + (1 - core)
    xs_at = [(x_at + dx) % HOPS for dx in (1, 3, 2)]
    ys_at = [(y_at + dy) % 4 for dy in (1, 3, 2)]
    across = (z_partner, (1 - z_hi) * 8 + y_at * 2 + core)

    def remote(src, dst, send, recv, at_cell, at_gene):
        return pltpu.make_async_remote_copy(
            src_ref=src, dst_ref=dst, send_sem=send, recv_sem=recv,
            device_id={"cell": at_cell, "gene": at_gene}, device_id_type=MESH,
        )

    tail = x_hbm.shape[1] - (cells - 1) * width

    def x_copy(d):
        lanes = tail if d == cells - 1 else width
        return pltpu.make_async_copy(
            x_hbm.at[:, pl.ds(d * width, lanes)], x.at[d, :, pl.ds(0, lanes)], x_sem.at[d]
        )

    for d in range(cells):
        x_copy(d).start()
    x[cells - 1, :, tail:] = jnp.zeros((x.shape[1], width - tail), x.dtype)

    barrier = pltpu.get_barrier_semaphore()
    greeted = [((cell + o) % cells, gene) for o in range(1, cells)]
    greeted += [(cell, z_hi * 8 + y_to * 2 + core) for y_to in ys_at]
    greeted += [across, (cell, core_partner)]
    for at_cell, at_gene in greeted:
        pl.semaphore_signal(
            barrier, inc=1, device_id={"cell": at_cell, "gene": at_gene}, device_id_type=MESH
        )
    pl.semaphore_wait(barrier, len(greeted))

    whole = at_ref[...].reshape(factors, -1)
    product = lax.dot_general(
        at_ref[z_hi, y_at, core], whole, (((1,), (1,)), ((), ())),
        preferred_element_type=jnp.float32,
    )
    gram_part[:pieces] = product.astype(jnp.bfloat16).reshape(pieces, 16, factors)
    gram_part[pieces:] = jnp.zeros_like(gram_part[pieces:])

    def gz_copy():
        src = gram_part.at[pl.ds((1 - z_lo) * HOPS, HOPS)]
        return remote(src, gram_z, gz_send, gz_recv, z_partner, gene)

    def gx_copy(x_to, slot):
        return remote(
            gram_mid.at[x_to], gram_x.at[slot], gx_send.at[x_to], gx_recv.at[slot],
            z_lo * HOPS + x_to, gene,
        )

    def hx_copy(x_to, slot):
        block = gram.at[z_hi, y_at, core, z_lo * HOPS + slot]
        return remote(
            block, block, hx_send.at[x_to], hx_recv.at[slot], z_lo * HOPS + x_to, gene
        )

    def hz_copy(side):
        block = gram.at[z_hi, y_at, core, pl.ds(side * HOPS, HOPS)]
        return remote(block, block, hz_send, hz_recv, z_partner, gene)

    gz_copy().start()

    for d in range(cells):
        x_copy(d).wait()

    def z1_copy(x_to):
        d = (1 - z_lo) * HOPS + x_to
        return remote(
            part.at[d, pl.ds(0, Z_ROWS)], z1.at[x_to], z1_send.at[x_to], z1_recv.at[x_to],
            z_partner, gene,
        )

    rest = pl.ds(Z_ROWS, factors - Z_ROWS)

    def x1_copy(z_to, x_to, slot):
        return remote(
            part.at[z_to * HOPS + x_to, rest], x1.at[slot, z_to],
            x1_send.at[x_to, z_to], x1_recv.at[slot, z_to], z_lo * HOPS + x_to, gene,
        )

    def x2_copy(x_to, slot):
        return remote(
            zs.at[x_to], x2.at[slot], x2_send.at[x_to], x2_recv.at[slot],
            z_lo * HOPS + x_to, gene,
        )

    def z2_copy():
        return remote(xs, z2, z2_send, z2_recv, z_partner, gene)

    def multiply(i, carry):
        x_to = (x_at + 1 + i) % HOPS
        z_to = (z_lo + 1 + i // HOPS) % 2
        d = z_to * HOPS + x_to
        value = jnp.dot(
            at_ref[...].reshape(factors, -1), x[d], preferred_element_type=jnp.float32
        )
        part[d] = value.astype(jnp.bfloat16)

        @pl.when(i < 2)
        def _():
            z1_copy(x_to).start()

        @pl.when((x_to != x_at) & (i != HELD))
        def _():
            x1_copy(z_to, x_to, x_at).start()

        return carry

    lax.fori_loop(0, HOPS, multiply, 0)

    gz_copy().wait_recv()
    mine = gram_part[pl.ds(z_lo * HOPS, HOPS)].astype(jnp.float32)
    gram_mid[...] = (mine + gram_z[...].astype(jnp.float32)).astype(jnp.bfloat16)
    for x_to in xs_at:
        gx_copy(x_to, x_at).start()

    lax.fori_loop(HOPS, cells, multiply, 0)

    def sq_copy(t, slot):
        return remote(squares.at[slot], squares.at[slot], sq_send.at[t], sq_recv.at[slot], t, gene)

    def square(b, total):
        value = at_ref[b // 8, b // 2 % 4, b % 2].astype(jnp.float32)
        return total + jnp.sum((value * value).reshape(-1, 8, value.shape[1]), axis=0)

    squares[cell] = lax.fori_loop(
        0, 16, square, jnp.zeros(squares.shape[1:], jnp.float32)
    )
    for o in range(1, cells):
        sq_copy((cell + o) % cells, cell).start()

    for b in range(relief_ref.shape[0]):
        rows = jnp.broadcast_to(relief_ref[b][None], (BLOCK // 8, 8, width))
        penalty[pl.ds(b * BLOCK, BLOCK)] = rows.reshape(BLOCK, width)

    def pair_sum(i):
        x_to = (x_at + 1 + i) % HOPS
        z1_copy(x_to).wait_recv()
        own = part[z_lo * HOPS + x_to, :Z_ROWS].astype(jnp.float32)
        zs[x_to] = (own + z1[x_to].astype(jnp.float32)).astype(jnp.bfloat16)
        if i < HOPS - 1:
            x2_copy(x_to, x_at).start()

    value = gram_mid[x_at].astype(jnp.float32)
    for slot in xs_at:
        gx_copy(x_at, slot).wait_recv()
        value = value + gram_x[slot].astype(jnp.float32)
    gram[z_hi, y_at, core, cell] = value.astype(jnp.bfloat16)
    for x_to in xs_at:
        hx_copy(x_to, x_at).start()
    x1_copy(z_lo, (x_at + 1 + HELD) % HOPS, x_at).start()

    pair_sum(0)

    for slot in xs_at:
        hx_copy(x_at, slot).wait_recv()
    hz_copy(z_lo).start()
    for i in range(2, HOPS):
        z1_copy((x_at + 1 + i) % HOPS).start()

    pair_sum(1)

    hz_copy(1 - z_lo).wait_recv()
    spread = Spread(
        gram, (z_hi, y_at, core), slice(0, HOPS), slice(HOPS, pieces),
        [(y_to, {"cell": cell, "gene": z_hi * 8 + y_to * 2 + core}) for y_to in ys_at],
        {"cell": across[0], "gene": across[1]}, {"cell": cell, "gene": core_partner},
        (gy_send, gy_recv, ga_send, ga_recv, own_send, own_recv),
        (fy_send, fy_recv, fz_send, fz_recv),
    )
    spread.begin()
    spread.relay_high()
    pair_sum(2)
    spread.relay_low()

    value = part[(1 - z_lo) * HOPS + x_at, Z_ROWS:].astype(jnp.float32)
    for o in range(1, HOPS):
        slot = (x_at + o) % HOPS
        x1_copy(1 - z_lo, x_at, slot).wait_recv()
        value = value + x1[slot, 1 - z_lo].astype(jnp.float32)
    xs[...] = value.astype(jnp.bfloat16)
    z2_copy().start()

    pair_sum(3)

    for o in range(1, cells):
        sq_copy(cell, (cell + o) % cells).wait_recv()
    sum_squares = jnp.sum(jnp.sum(squares[...], axis=0), keepdims=True)
    total_cells = cells * x.shape[1]
    step_size = 0.5 / (sum_squares / (total_cells * factors) + EPSILON)
    scale = step_size / total_cells
    inverse = 1.0 / (1.0 + step_size * RIDGE)

    def shrunk(moved, rows):
        limit = step_size * penalty[rows]
        return (jnp.maximum(moved - limit, 0.0) - jnp.maximum(-moved - limit, 0.0)) * inverse

    def start_from(value, rows):
        first[rows] = value
        start = shrunk(scale * value, rows)
        coef[rows] = start
        coef_bf[rows] = start.astype(jnp.bfloat16)

    for o in range(1, HOPS):
        slot = (x_at + o) % HOPS
        x2_copy(x_at, slot).wait_recv()
        x1_copy(z_lo, x_at, slot).wait_recv()

    def z_block(b, carry):
        rows = pl.ds(pl.multiple_of(b * BLOCK, BLOCK), BLOCK)
        value = zs[x_at, rows].astype(jnp.float32)
        for o in range(1, HOPS):
            value = value + x2[(x_at + o) % HOPS, rows].astype(jnp.float32)
        start_from(value, rows)
        return carry

    lax.fori_loop(0, Z_ROWS // BLOCK, z_block, 0)
    z2_copy().wait_recv()

    def x_block(b, carry):
        low = pl.ds(pl.multiple_of(b * BLOCK, BLOCK), BLOCK)
        rows = pl.ds(pl.multiple_of(b * BLOCK + Z_ROWS, BLOCK), BLOCK)
        value = part[cell, rows].astype(jnp.float32) + z2[low].astype(jnp.float32)
        for o in range(1, HOPS):
            value = value + x1[(x_at + o) % HOPS, z_lo, low].astype(jnp.float32)
        start_from(value, rows)
        return carry

    lax.fori_loop(0, (factors - Z_ROWS) // BLOCK, x_block, 0)

    spread.finish()
    height = out_ref.shape[1]

    def out_copy(t, slot):
        return remote(sent.at[t], out_ref.at[slot], out_send.at[t], out_recv.at[slot], t, gene)

    def finish(i, carry):
        t = (cell + 1 + i) % cells
        rows = pl.ds(pl.multiple_of(t * height, 32), height)
        block = gram[t // 4, t % 4, :, :pieces].reshape(height, factors)
        second = jnp.dot(block, coef_bf[...], preferred_element_type=jnp.float32)
        moved = coef[rows] - scale * (second - first[rows])
        value = (shrunk(moved, rows) * OUT_UNITS).astype(jnp.bfloat16)

        @pl.when(i < cells - 1)
        def _():
            sent[t] = value
            out_copy(t, cell).start()

        @pl.when(i == cells - 1)
        def _():
            out_ref[cell] = value

        return carry

    lax.fori_loop(0, cells, finish, 0)

    gz_copy().wait_send()
    hz_copy(z_lo).wait_send()
    for x_to in xs_at:
        gx_copy(x_to, x_at).wait_send()
        hx_copy(x_to, x_at).wait_send()
    spread.drain()

    for x_to in range(HOPS):
        z1_copy(x_to).wait_send()
    for o in range(1, HOPS):
        x_to = (x_at + o) % HOPS
        x2_copy(x_to, x_at).wait_send()
        for z_to in range(2):
            x1_copy(z_to, x_to, x_at).wait_send()
    z2_copy().wait_send()
    for o in range(1, cells):
        t = (cell + o) % cells
        sq_copy(t, cell).wait_send()
        out_copy(t, cell).wait_send()
        out_copy(cell, t).wait_recv()


def solve(activity_t, expression, block_mask):
    cell_devices, gene_devices = lax.axis_size("cell"), lax.axis_size("gene")
    own, cells = activity_t.shape[-2:]
    factors = gene_devices * own
    width = CHUNK
    gene_blocks, tf_blocks = block_mask.shape
    per = width // BLOCK
    relief = jnp.pad(block_mask.T.astype(jnp.float32), ((0, 0), (0, cell_devices * per - gene_blocks)))
    relief = lax.dynamic_slice_in_dim(relief, lax.axis_index("cell") * per, per, 1)
    relief = jnp.repeat(LASSO * (1.0 - PRIOR_RELIEF * relief), BLOCK, axis=1)
    relief = jnp.broadcast_to(relief[:, None], (tf_blocks, 8, width))
    rest = factors - Z_ROWS
    bf, f32 = jnp.bfloat16, jnp.float32
    vmem, dma = pltpu.VMEM, pltpu.SemaphoreType.DMA
    return pl.pallas_call(
        solve_kernel,
        out_shape=jax.ShapeDtypeStruct((cell_devices, factors // cell_devices, width), bf),
        in_specs=[
            pl.BlockSpec(memory_space=pltpu.VMEM),
            pl.BlockSpec(memory_space=pl.ANY),
            pl.BlockSpec(memory_space=pltpu.VMEM),
        ],
        out_specs=pl.BlockSpec(memory_space=pltpu.VMEM),
        scratch_shapes=[
            vmem((cell_devices, cells, width), bf),
            vmem((cell_devices, factors, width), bf),
            vmem((HOPS, Z_ROWS, width), bf),
            vmem((HOPS, Z_ROWS, width), bf),
            vmem((HOPS, 2, rest, width), bf),
            vmem((HOPS, Z_ROWS, width), bf),
            vmem((rest, width), bf),
            vmem((rest, width), bf),
            vmem((cell_devices, 16, factors), bf),
            vmem((HOPS, 16, factors), bf),
            vmem((HOPS, 16, factors), bf),
            vmem((HOPS, 16, factors), bf),
            vmem((2, 4, 2, cell_devices, 16, factors), bf),
            vmem((cell_devices, 8, cells), f32),
            vmem((factors, width), f32),
            vmem((factors, width), f32),
            vmem((factors, width), f32),
            vmem((factors, width), bf),
            vmem((cell_devices, factors // cell_devices, width), bf),
            dma((cell_devices,)),
            dma((HOPS,)), dma((HOPS,)),
            dma((HOPS, 2)), dma((HOPS, 2)),
            dma((HOPS,)), dma((HOPS,)),
            dma, dma,
            dma, dma, dma((HOPS,)), dma((HOPS,)), dma((HOPS,)), dma((HOPS,)), dma, dma,
            dma((2, 4)), dma((2, 4)), dma((2,)), dma((2,)), dma, dma,
            dma((2, 4)), dma((2, 4)), dma((2,)), dma((2,)),
            dma((cell_devices,)), dma((cell_devices,)),
            dma((cell_devices,)), dma((cell_devices,)),
        ],
        compiler_params=pltpu.CompilerParams(
            collective_id=1, has_side_effects=True, vmem_limit_bytes=60 * 2**20
        ),
        name="solve",
    )(activity_t, expression, relief)


def on_device(expression, prior_values, block_mask, gram_inverse):
    activity_t = activity_of(expression, prior_values, block_mask, gram_inverse)
    blocks = solve(activity_t, expression, block_mask)
    rows = blocks.shape[1]
    whole = blocks.transpose(1, 0, 2).reshape(rows, -1)
    return whole[:, : expression.shape[1]].astype(jnp.float32)


def solution(mesh):
    in_specs = (P("cell", "gene"), P("gene", None), P("gene", None), P(None, "gene"))
    out_specs = P("cell", "gene")
    return jax.shard_map(
        on_device, mesh=mesh, in_specs=in_specs, out_specs=out_specs, check_vma=False
    )
```

```python
import functools

import jax
import jax.numpy as jnp
from jax import lax
from jax.experimental import pallas as pl
from jax.experimental.pallas import tpu as pltpu
from jax.sharding import PartitionSpec as P

BLOCK = 128

OUT_UNITS = 100.0
LASSO = 0.006
RIDGE = 0.1
PRIOR_RELIEF = 0.7
EPSILON = 1e-06

MESH = pl.DeviceIdType.MESH
CHUNK = 256
SPLIT = 48
LAGS = (0, 1, 4, 7, 11, 15, 16)


class Spread:
    def __init__(self, ref, at, low, high, ys, across, partner, direct, handed):
        self.ref, (self.z, self.y, self.core) = ref, at
        self.rows = (low, high)
        self.ys, self.across, self.partner = ys, across, partner
        self.y_send, self.y_recv, self.z_send, self.z_recv, self.own_send, self.own_recv = direct
        self.fy_send, self.fy_recv, self.fz_send, self.fz_recv = handed

    def remote(self, block, send, recv, device):
        return pltpu.make_async_remote_copy(
            src_ref=block, dst_ref=block, send_sem=send, recv_sem=recv,
            device_id=device, device_id_type=MESH,
        )

    def own(self, side):
        block = self.ref.at[self.z, self.y, side]
        return self.remote(block, self.own_send, self.own_recv, self.partner)

    def over_y(self, k, device, y_to, slot):
        zs = slice(None) if k else self.z
        block = self.ref.at[zs, slot, self.core, self.rows[k]]
        return self.remote(block, self.y_send.at[k, y_to], self.y_recv.at[k, slot], device)

    def over_z(self, k, side):
        ys = self.y if k else slice(None)
        block = self.ref.at[side, ys, self.core, self.rows[k]]
        return self.remote(block, self.z_send.at[k], self.z_recv.at[k], self.across)

    def hand_y(self, k, slot, side):
        zs = slice(None) if k else self.z
        block = self.ref.at[zs, slot, side, self.rows[k]]
        return self.remote(block, self.fy_send.at[k, slot], self.fy_recv.at[k, slot], self.partner)

    def hand_z(self, k, side):
        ys = self.y if k else slice(None)
        block = self.ref.at[1 - self.z, ys, side, self.rows[k]]
        return self.remote(block, self.fz_send.at[k], self.fz_recv.at[k], self.partner)

    def begin(self):
        self.over_z(1, self.z).start()
        for y_to, device in self.ys:
            self.over_y(0, device, y_to, self.y).start()
        self.own(self.core).start()

    def relay_high(self):
        self.over_z(1, 1 - self.z).wait_recv()
        for y_to, device in self.ys:
            self.over_y(1, device, y_to, self.y).start()
        self.hand_z(1, self.core).start()

    def relay_low(self):
        for slot, device in self.ys:
            self.over_y(0, device, self.y, slot).wait_recv()
        self.over_z(0, self.z).start()
        for slot, _ in self.ys:
            self.hand_y(0, slot, self.core).start()

    def finish(self):
        for slot, device in self.ys:
            self.over_y(1, device, self.y, slot).wait_recv()
            self.hand_y(1, slot, self.core).start()
        self.over_z(0, 1 - self.z).wait_recv()
        self.hand_z(0, self.core).start()
        self.own(1 - self.core).wait_recv()
        for k in range(2):
            self.hand_z(k, 1 - self.core).wait_recv()
            for slot, _ in self.ys:
                self.hand_y(k, slot, 1 - self.core).wait_recv()

    def drain(self):
        self.own(self.core).wait_send()
        for k in range(2):
            self.over_z(k, self.z).wait_send()
            self.hand_z(k, self.core).wait_send()
            for y_to, device in self.ys:
                self.over_y(k, device, y_to, self.y).wait_send()
                self.hand_y(k, y_to, self.core).wait_send()


def activity_kernel(
    x_hbm, prior_hbm, mask_ref, gram_ref, at_ref,
    x, prior, support, part, pair, total, near_z, near_y, mid_z, mid_y, last_z, last_y, scores, acc,
    x_sem, prior_sem, pair_send, pair_recv,
    rs_y_send, rs_y_recv, rs_z_send, rs_z_recv,
    ag_y_send, ag_y_recv, ag_z_send, ag_z_recv, fw_send, fw_recv,
    at_y_send, at_y_recv, at_z_send, at_z_recv, own_send, own_recv,
    af_y_send, af_y_recv, af_z_send, af_z_recv,
):
    chunks, genes, _ = prior.shape
    me = lax.axis_index("gene")
    core, y, z = me % 2, (me // 2) % 4, me // 8
    partner = z * 8 + y * 2 + (1 - core)
    across = (1 - z) * 8 + y * 2 + core
    turns = (1, 3, 2)
    ys = [(y + dy) % 4 for dy in turns]

    x_copy = pltpu.make_async_copy(x_hbm, x, x_sem)

    def prior_copy(n):
        columns = pl.ds(pl.multiple_of(n * CHUNK, CHUNK), CHUNK)
        return pltpu.make_async_copy(prior_hbm.at[:, columns], prior.at[n], prior_sem.at[n])

    prior_copy(0).start()
    x_copy.start()
    for n in range(1, chunks):
        prior_copy(n).start()

    def device_of(y_to):
        return z * 8 + y_to * 2 + core

    barrier = pltpu.get_barrier_semaphore()
    for device in [device_of(y_to) for y_to in ys] + [across, partner]:
        pl.semaphore_signal(barrier, inc=1, device_id={"gene": device}, device_id_type=MESH)
    pl.semaphore_wait(barrier, len(ys) + 2)

    for b in range(mask_ref.shape[1]):
        lanes = slice(b % 2 * BLOCK, b % 2 * BLOCK + BLOCK)
        support[b // 2, :, lanes] = jnp.broadcast_to(
            mask_ref[:, b : b + 1].astype(jnp.float32), (support.shape[1], BLOCK)
        )

    def remote(src, dst, send, recv, device):
        return pltpu.make_async_remote_copy(
            src_ref=src, dst_ref=dst, send_sem=send, recv_sem=recv,
            device_id={"gene": device}, device_id_type=MESH,
        )

    def pair_copy(n):
        return remote(
            part.at[n, :, :, 1 - core], pair.at[n], pair_send.at[n], pair_recv.at[n], partner
        )

    def rs_y(n, z_first, y_to, slot):
        if z_first:
            src, dst = mid_z.at[n, y_to], last_z.at[n, slot]
        else:
            src, dst = total.at[n, :, y_to], near_y.at[n, slot]
        return remote(src, dst, rs_y_send.at[n, y_to], rs_y_recv.at[n, slot], device_of(y_to))

    def rs_z(n, z_first):
        if z_first:
            src, dst = total.at[n, 1 - z], near_z.at[n]
        else:
            src, dst = mid_y.at[n, 1 - z], last_y.at[n]
        return remote(src, dst, rs_z_send.at[n], rs_z_recv.at[n], across)

    def ag_y(n, z_first, y_to, slot):
        block = scores.at[n, :, slot, core] if z_first else scores.at[n, z, slot, core]
        return remote(
            block, block, ag_y_send.at[n, y_to], ag_y_recv.at[n, slot], device_of(y_to)
        )

    def ag_z(n, z_first, side):
        block = scores.at[n, side, y, core] if z_first else scores.at[n, side, :, core]
        return remote(block, block, ag_z_send.at[n], ag_z_recv.at[n], across)

    def fw_copy(n, side):
        block = scores.at[n, :, :, side]
        return remote(block, block, fw_send.at[n], fw_recv.at[n], partner)

    def wide(value):
        return value.astype(jnp.float32)

    def by_order(n, parity, step):
        @pl.when(n % 2 == parity)
        def _():
            step(True)

        @pl.when(n % 2 != parity)
        def _():
            step(False)

    def multiply(n):
        prior_copy(n).wait()

        rows = jnp.broadcast_to(support[n][:, None], (support.shape[1], 16, CHUNK))
        masked = prior[n].reshape(-1, BLOCK // 16, 16, CHUNK) * rows.astype(jnp.bfloat16)[:, None]
        prior[n] = masked.reshape(prior.shape[1:])
        product = jnp.dot(x[...], prior[n], preferred_element_type=jnp.float32)
        part[n] = product.astype(jnp.bfloat16).reshape(part.shape[1:])
        pair_copy(n).start()

    def spread(n):
        pair_copy(n).wait_recv()
        total[n] = (wide(part[n, :, :, core]) + wide(pair[n])).astype(jnp.bfloat16)

        def step(z_first):
            if z_first:
                rs_z(n, True).start()
            else:
                for y_to in ys:
                    rs_y(n, False, y_to, y).start()

        by_order(n, 0, step)

    def middle(n):
        def step(z_first):
            if z_first:
                rs_z(n, True).wait_recv()
                mid_z[n] = (wide(total[n, z]) + wide(near_z[n])).astype(jnp.bfloat16)
                for y_to in ys:
                    rs_y(n, True, y_to, y).start()
            else:
                value = wide(total[n, :, y])
                for slot in ys:
                    rs_y(n, False, y, slot).wait_recv()
                    value = value + wide(near_y[n, slot])
                mid_y[n] = value.astype(jnp.bfloat16)
                rs_z(n, False).start()

        by_order(n, 0, step)

    def collect(n):
        def step(z_first):
            if z_first:
                value = wide(mid_z[n, y])
                for slot in ys:
                    rs_y(n, True, y, slot).wait_recv()
                    value = value + wide(last_z[n, slot])
            else:
                rs_z(n, False).wait_recv()
                value = wide(mid_y[n, z]) + wide(last_y[n])
            scores[n, z, y, core] = value.astype(jnp.bfloat16)

        by_order(n, 0, step)

        def out(z_first):
            if z_first:
                ag_z(n, True, z).start()
            else:
                for y_to in ys:
                    ag_y(n, False, y_to, y).start()

        by_order(n, 1, out)

    def relay(n):
        def step(z_first):
            if z_first:
                ag_z(n, True, 1 - z).wait_recv()
                for y_to in ys:
                    ag_y(n, True, y_to, y).start()
            else:
                for slot in ys:
                    ag_y(n, False, y, slot).wait_recv()
                ag_z(n, False, z).start()

        by_order(n, 1, step)

    def share(n):
        def step(z_first):
            if z_first:
                for slot in ys:
                    ag_y(n, True, y, slot).wait_recv()
            else:
                ag_z(n, False, 1 - z).wait_recv()

        by_order(n, 1, step)
        fw_copy(n, core).start()

    acc[...] = jnp.zeros_like(acc)

    def mix(n):
        fw_copy(n, 1 - core).wait_recv()
        lanes = pl.ds(pl.multiple_of(n * CHUNK, CHUNK), CHUNK)
        acc[...] += lax.dot_general(
            gram_ref[:, lanes], scores[n].reshape(-1, CHUNK), (((1,), (1,)), ((), ())),
            preferred_element_type=jnp.float32,
        )

    x_copy.wait()
    stages = (
        (LAGS[0], multiply), (LAGS[1], spread), (LAGS[2], middle), (LAGS[3], collect),
        (LAGS[4], relay), (LAGS[5], share), (LAGS[6], mix),
    )

    def turn(i, carry):
        for lag, stage in stages:
            @pl.when((i >= lag) & (i < lag + chunks))
            def _():
                stage(i - lag)

        return carry

    lax.fori_loop(0, chunks + LAGS[-1], turn, 0)

    at_ref[z, y, core] = acc[...].astype(jnp.bfloat16)
    spread_at = Spread(
        at_ref, (z, y, core), slice(0, SPLIT), slice(SPLIT, at_ref.shape[3]),
        [(y_to, {"gene": device_of(y_to)}) for y_to in ys], {"gene": across}, {"gene": partner},
        (at_y_send, at_y_recv, at_z_send, at_z_recv, own_send, own_recv),
        (af_y_send, af_y_recv, af_z_send, af_z_recv),
    )
    spread_at.begin()
    spread_at.relay_high()
    spread_at.relay_low()
    spread_at.finish()

    def drain(n, carry):
        pair_copy(n).wait_send()
        fw_copy(n, core).wait_send()

        def reduced(z_first):
            rs_z(n, z_first).wait_send()
            for y_to in ys:
                rs_y(n, z_first, y_to, y).wait_send()

        by_order(n, 0, reduced)

        def gathered(z_first):
            ag_z(n, z_first, z).wait_send()
            for y_to in ys:
                ag_y(n, z_first, y_to, y).wait_send()

        by_order(n, 1, gathered)
        return carry

    lax.fori_loop(0, chunks, drain, 0)
    spread_at.drain()


def activity_of(expression, prior_values, block_mask, gram_inverse):
    devices = lax.axis_size("gene")
    cells, genes = expression.shape
    factors = prior_values.shape[1]
    own = gram_inverse.shape[1]
    chunks = factors // CHUNK
    rows = cells // devices
    bf = jnp.bfloat16
    vmem, dma = pltpu.VMEM, pltpu.SemaphoreType.DMA
    blocks = pl.pallas_call(
        activity_kernel,
        out_shape=jax.ShapeDtypeStruct((2, 4, 2, own, cells), bf),
        in_specs=[pl.BlockSpec(memory_space=pl.ANY)] * 2
        + [pl.BlockSpec(memory_space=pltpu.VMEM)] * 2,
        out_specs=pl.BlockSpec(memory_space=pltpu.VMEM),
        scratch_shapes=[
            vmem((cells, genes), bf),
            vmem((chunks, genes, CHUNK), bf),
            vmem((chunks, genes // BLOCK, CHUNK), jnp.float32),
            vmem((chunks, 2, 4, 2, rows, CHUNK), bf),
            vmem((chunks, 2, 4, rows, CHUNK), bf),
            vmem((chunks, 2, 4, rows, CHUNK), bf),
            vmem((chunks, 4, rows, CHUNK), bf),
            vmem((chunks, 4, 2, rows, CHUNK), bf),
            vmem((chunks, 4, rows, CHUNK), bf),
            vmem((chunks, 2, rows, CHUNK), bf),
            vmem((chunks, 4, rows, CHUNK), bf),
            vmem((chunks, rows, CHUNK), bf),
            vmem((chunks, 2, 4, 2, rows, CHUNK), bf),
            vmem((own, cells), jnp.float32),
            dma, dma((chunks,)), dma((chunks,)), dma((chunks,)),
            dma((chunks, 4)), dma((chunks, 4)), dma((chunks,)), dma((chunks,)),
            dma((chunks, 4)), dma((chunks, 4)), dma((chunks,)), dma((chunks,)),
            dma((chunks,)), dma((chunks,)),
            dma((2, 4)), dma((2, 4)), dma((2,)), dma((2,)), dma, dma,
            dma((2, 4)), dma((2, 4)), dma((2,)), dma((2,)),
        ],
        compiler_params=pltpu.CompilerParams(
            collective_id=0, has_side_effects=True, vmem_limit_bytes=56 * 2**20
        ),
        name="activity",
    )(expression, prior_values, block_mask, gram_inverse.T)
    return blocks


Z_ROWS = 768
HOPS = 4


def solve_kernel(
    at_ref, x_hbm, relief_ref, out_ref,
    x, part, z1, zs, r1, x1, r2, x2, xs, z2, gram_part, gram_z, gram_mid, gram_x, gram, squares, penalty,
    first, coef, coef_bf, sent,
    x_sem, z1_send, z1_recv, r1_send, r1_recv, x1_send, x1_recv, r2_send, r2_recv,
    x2_send, x2_recv, z2_send, z2_recv,
    gz_send, gz_recv, gx_send, gx_recv, hx_send, hx_recv, hz_send, hz_recv,
    gy_send, gy_recv, ga_send, ga_recv, own_send, own_recv, fy_send, fy_recv, fz_send, fz_recv,
    sq_send, sq_recv, out_send, out_recv,
):
    cells = 2 * HOPS
    pieces = at_ref.shape[3] // 16
    factors, width = first.shape
    cell, gene = lax.axis_index("cell"), lax.axis_index("gene")
    x_at, z_lo = cell % HOPS, cell // HOPS
    core, y_at, z_hi = gene % 2, (gene // 2) % 4, gene // 8
    z_partner = (1 - z_lo) * HOPS + x_at
    core_partner = z_hi * 8 + y_at * 2 + (1 - core)
    right, left, far = [(x_at + dx) % HOPS for dx in (1, 3, 2)]
    xs_at = [right, left, far]
    ys_at = [(y_at + dy) % 4 for dy in (1, 3, 2)]
    across = (z_partner, (1 - z_hi) * 8 + y_at * 2 + core)

    def remote(src, dst, send, recv, at_cell, at_gene):
        return pltpu.make_async_remote_copy(
            src_ref=src, dst_ref=dst, send_sem=send, recv_sem=recv,
            device_id={"cell": at_cell, "gene": at_gene}, device_id_type=MESH,
        )

    tail = x_hbm.shape[1] - (cells - 1) * width

    def x_copy(d):
        lanes = tail if d == cells - 1 else width
        return pltpu.make_async_copy(
            x_hbm.at[:, pl.ds(d * width, lanes)], x.at[d, :, pl.ds(0, lanes)], x_sem.at[d]
        )

    for d in range(cells):
        x_copy(d).start()
    x[cells - 1, :, tail:] = jnp.zeros((x.shape[1], width - tail), x.dtype)

    barrier = pltpu.get_barrier_semaphore()
    greeted = [((cell + o) % cells, gene) for o in range(1, cells)]
    greeted += [(cell, z_hi * 8 + y_to * 2 + core) for y_to in ys_at]
    greeted += [across, (cell, core_partner)]
    for at_cell, at_gene in greeted:
        pl.semaphore_signal(
            barrier, inc=1, device_id={"cell": at_cell, "gene": at_gene}, device_id_type=MESH
        )
    pl.semaphore_wait(barrier, len(greeted))

    whole = at_ref[...].reshape(factors, -1)
    product = lax.dot_general(
        at_ref[z_hi, y_at, core], whole, (((1,), (1,)), ((), ())),
        preferred_element_type=jnp.float32,
    )
    gram_part[:pieces] = product.astype(jnp.bfloat16).reshape(pieces, 16, factors)
    gram_part[pieces:] = jnp.zeros_like(gram_part[pieces:])

    def gz_copy():
        src = gram_part.at[pl.ds((1 - z_lo) * HOPS, HOPS)]
        return remote(src, gram_z, gz_send, gz_recv, z_partner, gene)

    def gx_copy(x_to, slot):
        return remote(
            gram_mid.at[x_to], gram_x.at[slot], gx_send.at[x_to], gx_recv.at[slot],
            z_lo * HOPS + x_to, gene,
        )

    def hx_copy(x_to, slot):
        block = gram.at[z_hi, y_at, core, z_lo * HOPS + slot]
        return remote(
            block, block, hx_send.at[x_to], hx_recv.at[slot], z_lo * HOPS + x_to, gene
        )

    def hz_copy(side):
        block = gram.at[z_hi, y_at, core, pl.ds(side * HOPS, HOPS)]
        return remote(block, block, hz_send, hz_recv, z_partner, gene)

    gz_copy().start()

    for d in range(cells):
        x_copy(d).wait()

    def z1_copy(x_to):
        d = (1 - z_lo) * HOPS + x_to
        return remote(
            part.at[d, pl.ds(0, Z_ROWS)], z1.at[x_to], z1_send.at[x_to], z1_recv.at[x_to],
            z_partner, gene,
        )

    rest = pl.ds(Z_ROWS, factors - Z_ROWS)

    def toward(k):
        return z_lo * HOPS + (left if k else right)

    def r1_copy(k):
        z_to = z_lo if k else 1 - z_lo
        return remote(
            part.at[z_to * HOPS + far, rest], r1.at[k], r1_send.at[k], r1_recv.at[k],
            toward(k), gene,
        )

    def x1_copy(z_to, k):
        return remote(
            part.at[z_to * HOPS + (left if k else right), rest], x1.at[z_to, k],
            x1_send.at[z_to, k], x1_recv.at[z_to, k], toward(k), gene,
        )

    def pass_on(k):
        z_to = z_lo if k else 1 - z_lo
        d = z_to * HOPS + (left if k else right)
        r1_copy(k).wait_recv()
        value = part[d, Z_ROWS:].astype(jnp.float32) + r1[k].astype(jnp.float32)
        part[d, Z_ROWS:] = value.astype(jnp.bfloat16)
        x1_copy(z_to, k).start()

    half = Z_ROWS // 2

    def r2_copy(k):
        return remote(
            zs.at[far, pl.ds(k * half, half)], r2.at[k], r2_send.at[k], r2_recv.at[k],
            toward(k), gene,
        )

    def x2_copy(k):
        return remote(
            zs.at[left if k else right], x2.at[k], x2_send.at[k], x2_recv.at[k], toward(k), gene
        )

    def z2_copy():
        return remote(xs, z2, z2_send, z2_recv, z_partner, gene)

    def order(i):
        return (x_at + 2 - i + (i // 2) * (2 * i - 1)) % HOPS

    def multiply(i, carry):
        x_to = order(i % HOPS)
        z_to = (z_lo + 1 + i // HOPS) % 2
        d = z_to * HOPS + x_to
        value = jnp.dot(
            at_ref[...].reshape(factors, -1), x[d], preferred_element_type=jnp.float32
        )
        part[d] = value.astype(jnp.bfloat16)

        @pl.when(i < 2)
        def _():
            z1_copy(x_to).start()

        @pl.when(i == 0)
        def _():
            r1_copy(0).start()

        @pl.when(i == 2)
        def _():
            x1_copy(1 - z_lo, 1).start()

        return carry

    lax.fori_loop(0, HOPS, multiply, 0)

    gz_copy().wait_recv()
    mine = gram_part[pl.ds(z_lo * HOPS, HOPS)].astype(jnp.float32)
    gram_mid[...] = (mine + gram_z[...].astype(jnp.float32)).astype(jnp.bfloat16)
    for x_to in xs_at:
        gx_copy(x_to, x_at).start()

    lax.fori_loop(HOPS, cells, multiply, 0)

    def sq_copy(t, slot):
        return remote(squares.at[slot], squares.at[slot], sq_send.at[t], sq_recv.at[slot], t, gene)

    def square(b, total):
        value = at_ref[b // 8, b // 2 % 4, b % 2].astype(jnp.float32)
        return total + jnp.sum((value * value).reshape(-1, 8, value.shape[1]), axis=0)

    squares[cell] = lax.fori_loop(
        0, 16, square, jnp.zeros(squares.shape[1:], jnp.float32)
    )
    for o in range(1, cells):
        sq_copy((cell + o) % cells, cell).start()

    for b in range(relief_ref.shape[0]):
        rows = jnp.broadcast_to(relief_ref[b][None], (BLOCK // 8, 8, width))
        penalty[pl.ds(b * BLOCK, BLOCK)] = rows.reshape(BLOCK, width)

    def pair_sum(i):
        x_to = order(i)
        z1_copy(x_to).wait_recv()
        own = part[z_lo * HOPS + x_to, :Z_ROWS].astype(jnp.float32)
        value = own + z1[x_to].astype(jnp.float32)
        zs[x_to] = value.astype(jnp.bfloat16)
        if i == 0:
            r2_copy(0).start()
            r2_copy(1).start()
        elif i < HOPS - 1:
            k = i - 1
            rows = pl.ds(k * half, half)
            r2_copy(k).wait_recv()
            value = zs[x_to, rows].astype(jnp.float32) + r2[k].astype(jnp.float32)
            zs[x_to, rows] = value.astype(jnp.bfloat16)
            x2_copy(k).start()

    value = gram_mid[x_at].astype(jnp.float32)
    for slot in xs_at:
        gx_copy(x_at, slot).wait_recv()
        value = value + gram_x[slot].astype(jnp.float32)
    gram[z_hi, y_at, core, cell] = value.astype(jnp.bfloat16)
    for x_to in xs_at:
        hx_copy(x_to, x_at).start()
    r1_copy(1).start()
    pass_on(0)
    pair_sum(0)
    x1_copy(z_lo, 0).start()

    for slot in xs_at:
        hx_copy(x_at, slot).wait_recv()
    hz_copy(z_lo).start()
    for i in range(2, HOPS):
        z1_copy(order(i)).start()

    hz_copy(1 - z_lo).wait_recv()
    spread = Spread(
        gram, (z_hi, y_at, core), slice(0, HOPS), slice(HOPS, pieces),
        [(y_to, {"cell": cell, "gene": z_hi * 8 + y_to * 2 + core}) for y_to in ys_at],
        {"cell": across[0], "gene": across[1]}, {"cell": cell, "gene": core_partner},
        (gy_send, gy_recv, ga_send, ga_recv, own_send, own_recv),
        (fy_send, fy_recv, fz_send, fz_recv),
    )
    spread.begin()
    pass_on(1)
    spread.relay_high()
    pair_sum(1)
    pair_sum(2)

    value = part[(1 - z_lo) * HOPS + x_at, Z_ROWS:].astype(jnp.float32)
    for k in range(2):
        x1_copy(1 - z_lo, k).wait_recv()
        value = value + x1[1 - z_lo, k].astype(jnp.float32)
    xs[...] = value.astype(jnp.bfloat16)
    z2_copy().start()
    spread.relay_low()
    pair_sum(3)

    for o in range(1, cells):
        sq_copy(cell, (cell + o) % cells).wait_recv()
    sum_squares = jnp.sum(jnp.sum(squares[...], axis=0), keepdims=True)
    total_cells = cells * x.shape[1]
    step_size = 0.5 / (sum_squares / (total_cells * factors) + EPSILON)
    scale = step_size / total_cells
    inverse = 1.0 / (1.0 + step_size * RIDGE)

    def shrunk(moved, rows):
        limit = step_size * penalty[rows]
        return (jnp.maximum(moved - limit, 0.0) - jnp.maximum(-moved - limit, 0.0)) * inverse

    def start_from(value, rows):
        first[rows] = value
        start = shrunk(scale * value, rows)
        coef[rows] = start
        coef_bf[rows] = start.astype(jnp.bfloat16)

    for k in range(2):
        x2_copy(k).wait_recv()
        x1_copy(z_lo, k).wait_recv()

    def z_block(b, carry):
        rows = pl.ds(pl.multiple_of(b * BLOCK, BLOCK), BLOCK)
        value = zs[x_at, rows].astype(jnp.float32)
        for k in range(2):
            value = value + x2[k, rows].astype(jnp.float32)
        start_from(value, rows)
        return carry

    lax.fori_loop(0, Z_ROWS // BLOCK, z_block, 0)
    z2_copy().wait_recv()

    def x_block(b, carry):
        low = pl.ds(pl.multiple_of(b * BLOCK, BLOCK), BLOCK)
        rows = pl.ds(pl.multiple_of(b * BLOCK + Z_ROWS, BLOCK), BLOCK)
        value = part[cell, rows].astype(jnp.float32) + z2[low].astype(jnp.float32)
        for k in range(2):
            value = value + x1[z_lo, k, low].astype(jnp.float32)
        start_from(value, rows)
        return carry

    lax.fori_loop(0, (factors - Z_ROWS) // BLOCK, x_block, 0)

    spread.finish()
    height = out_ref.shape[1]

    def out_copy(t, slot):
        return remote(sent.at[t], out_ref.at[slot], out_send.at[t], out_recv.at[slot], t, gene)

    def finish(i, carry):
        p = (cell // 2 + 1 + i) % HOPS
        rows = pl.ds(pl.multiple_of(p * (2 * height), 64), 2 * height)
        block = gram[p // 2, pl.ds(p % 2 * 2, 2), :, :pieces].reshape(2 * height, factors)
        second = jnp.dot(block, coef_bf[...], preferred_element_type=jnp.float32)
        moved = coef[rows] - scale * (second - first[rows])
        value = (shrunk(moved, rows) * OUT_UNITS).astype(jnp.bfloat16)
        for h in range(2):
            t = 2 * p + h
            piece = value[h * height : (h + 1) * height]

            @pl.when(t != cell)
            def _():
                sent[t] = piece
                out_copy(t, cell).start()

            @pl.when(t == cell)
            def _():
                out_ref[cell] = piece

        return carry

    lax.fori_loop(0, HOPS, finish, 0)

    gz_copy().wait_send()
    hz_copy(z_lo).wait_send()
    for x_to in xs_at:
        gx_copy(x_to, x_at).wait_send()
        hx_copy(x_to, x_at).wait_send()
    spread.drain()

    for x_to in range(HOPS):
        z1_copy(x_to).wait_send()
    for k in range(2):
        r1_copy(k).wait_send()
        r2_copy(k).wait_send()
        x2_copy(k).wait_send()
        for z_to in range(2):
            x1_copy(z_to, k).wait_send()
    z2_copy().wait_send()
    for o in range(1, cells):
        t = (cell + o) % cells
        sq_copy(t, cell).wait_send()
        out_copy(t, cell).wait_send()
        out_copy(cell, t).wait_recv()


def solve(activity_t, expression, block_mask):
    cell_devices, gene_devices = lax.axis_size("cell"), lax.axis_size("gene")
    own, cells = activity_t.shape[-2:]
    factors = gene_devices * own
    width = CHUNK
    gene_blocks, tf_blocks = block_mask.shape
    per = width // BLOCK
    relief = jnp.pad(block_mask.T.astype(jnp.float32), ((0, 0), (0, cell_devices * per - gene_blocks)))
    relief = lax.dynamic_slice_in_dim(relief, lax.axis_index("cell") * per, per, 1)
    relief = jnp.repeat(LASSO * (1.0 - PRIOR_RELIEF * relief), BLOCK, axis=1)
    relief = jnp.broadcast_to(relief[:, None], (tf_blocks, 8, width))
    rest = factors - Z_ROWS
    bf, f32 = jnp.bfloat16, jnp.float32
    vmem, dma = pltpu.VMEM, pltpu.SemaphoreType.DMA
    return pl.pallas_call(
        solve_kernel,
        out_shape=jax.ShapeDtypeStruct((cell_devices, factors // cell_devices, width), bf),
        in_specs=[
            pl.BlockSpec(memory_space=pltpu.VMEM),
            pl.BlockSpec(memory_space=pl.ANY),
            pl.BlockSpec(memory_space=pltpu.VMEM),
        ],
        out_specs=pl.BlockSpec(memory_space=pltpu.VMEM),
        scratch_shapes=[
            vmem((cell_devices, cells, width), bf),
            vmem((cell_devices, factors, width), bf),
            vmem((HOPS, Z_ROWS, width), bf),
            vmem((HOPS, Z_ROWS, width), bf),
            vmem((2, rest, width), bf),
            vmem((2, 2, rest, width), bf),
            vmem((2, Z_ROWS // 2, width), bf),
            vmem((2, Z_ROWS, width), bf),
            vmem((rest, width), bf),
            vmem((rest, width), bf),
            vmem((cell_devices, 16, factors), bf),
            vmem((HOPS, 16, factors), bf),
            vmem((HOPS, 16, factors), bf),
            vmem((HOPS, 16, factors), bf),
            vmem((2, 4, 2, cell_devices, 16, factors), bf),
            vmem((cell_devices, 8, cells), f32),
            vmem((factors, width), f32),
            vmem((factors, width), f32),
            vmem((factors, width), f32),
            vmem((factors, width), bf),
            vmem((cell_devices, factors // cell_devices, width), bf),
            dma((cell_devices,)),
            dma((HOPS,)), dma((HOPS,)),
            dma((2,)), dma((2,)), dma((2, 2)), dma((2, 2)),
            dma((2,)), dma((2,)), dma((2,)), dma((2,)),
            dma, dma,
            dma, dma, dma((HOPS,)), dma((HOPS,)), dma((HOPS,)), dma((HOPS,)), dma, dma,
            dma((2, 4)), dma((2, 4)), dma((2,)), dma((2,)), dma, dma,
            dma((2, 4)), dma((2, 4)), dma((2,)), dma((2,)),
            dma((cell_devices,)), dma((cell_devices,)),
            dma((cell_devices,)), dma((cell_devices,)),
        ],
        compiler_params=pltpu.CompilerParams(
            collective_id=1, has_side_effects=True, vmem_limit_bytes=60 * 2**20
        ),
        name="solve",
    )(activity_t, expression, relief)


def on_device(expression, prior_values, block_mask, gram_inverse):
    activity_t = activity_of(expression, prior_values, block_mask, gram_inverse)
    blocks = solve(activity_t, expression, block_mask)
    rows = blocks.shape[1]
    whole = blocks.transpose(1, 0, 2).reshape(rows, -1)
    return whole[:, : expression.shape[1]].astype(jnp.float32)


def solution(mesh):
    in_specs = (P("cell", "gene"), P("gene", None), P("gene", None), P(None, "gene"))
    out_specs = P("cell", "gene")
    return jax.shard_map(
        on_device, mesh=mesh, in_specs=in_specs, out_specs=out_specs, check_vma=False
    )
```

```python
import functools

import jax
import jax.numpy as jnp
from jax import lax
from jax.experimental import pallas as pl
from jax.experimental.pallas import tpu as pltpu
from jax.sharding import PartitionSpec as P

BLOCK = 128

OUT_UNITS = 100.0
LASSO = 0.006
RIDGE = 0.1
PRIOR_RELIEF = 0.7
EPSILON = 1e-06

MESH = pl.DeviceIdType.MESH
CHUNK = 256
SPLIT = 48
LAGS = (0, 1, 4, 7, 11, 15, 16)


class Spread:
    def __init__(self, ref, at, low, high, ys, across, partner, direct, handed):
        self.ref, (self.z, self.y, self.core) = ref, at
        self.rows = (low, high)
        self.ys, self.across, self.partner = ys, across, partner
        self.y_send, self.y_recv, self.z_send, self.z_recv, self.own_send, self.own_recv = direct
        self.fy_send, self.fy_recv, self.fz_send, self.fz_recv = handed

    def remote(self, block, send, recv, device):
        return pltpu.make_async_remote_copy(
            src_ref=block, dst_ref=block, send_sem=send, recv_sem=recv,
            device_id=device, device_id_type=MESH,
        )

    def own(self, side):
        block = self.ref.at[self.z, self.y, side]
        return self.remote(block, self.own_send, self.own_recv, self.partner)

    def over_y(self, k, device, y_to, slot):
        zs = slice(None) if k else self.z
        block = self.ref.at[zs, slot, self.core, self.rows[k]]
        return self.remote(block, self.y_send.at[k, y_to], self.y_recv.at[k, slot], device)

    def over_z(self, k, side):
        ys = self.y if k else slice(None)
        block = self.ref.at[side, ys, self.core, self.rows[k]]
        return self.remote(block, self.z_send.at[k], self.z_recv.at[k], self.across)

    def hand_y(self, k, slot, side):
        zs = slice(None) if k else self.z
        block = self.ref.at[zs, slot, side, self.rows[k]]
        return self.remote(block, self.fy_send.at[k, slot], self.fy_recv.at[k, slot], self.partner)

    def hand_z(self, k, side):
        ys = self.y if k else slice(None)
        block = self.ref.at[1 - self.z, ys, side, self.rows[k]]
        return self.remote(block, self.fz_send.at[k], self.fz_recv.at[k], self.partner)

    def begin(self):
        self.over_z(1, self.z).start()
        for y_to, device in self.ys:
            self.over_y(0, device, y_to, self.y).start()
        self.own(self.core).start()

    def relay_high(self):
        self.over_z(1, 1 - self.z).wait_recv()
        for y_to, device in self.ys:
            self.over_y(1, device, y_to, self.y).start()
        self.hand_z(1, self.core).start()

    def relay_low(self):
        for slot, device in self.ys:
            self.over_y(0, device, self.y, slot).wait_recv()
        self.over_z(0, self.z).start()
        for slot, _ in self.ys:
            self.hand_y(0, slot, self.core).start()

    def finish(self):
        for slot, device in self.ys:
            self.over_y(1, device, self.y, slot).wait_recv()
            self.hand_y(1, slot, self.core).start()
        self.over_z(0, 1 - self.z).wait_recv()
        self.hand_z(0, self.core).start()
        self.own(1 - self.core).wait_recv()
        for k in range(2):
            self.hand_z(k, 1 - self.core).wait_recv()
            for slot, _ in self.ys:
                self.hand_y(k, slot, 1 - self.core).wait_recv()

    def drain(self):
        self.own(self.core).wait_send()
        for k in range(2):
            self.over_z(k, self.z).wait_send()
            self.hand_z(k, self.core).wait_send()
            for y_to, device in self.ys:
                self.over_y(k, device, y_to, self.y).wait_send()
                self.hand_y(k, y_to, self.core).wait_send()


def activity_kernel(
    x_hbm, prior_hbm, mask_ref, gram_ref, at_ref,
    x, prior, support, part, pair, total, near_z, near_y, mid_z, mid_y, last_z, last_y, scores, acc,
    x_sem, prior_sem, pair_send, pair_recv,
    rs_y_send, rs_y_recv, rs_z_send, rs_z_recv,
    ag_y_send, ag_y_recv, ag_z_send, ag_z_recv, fw_send, fw_recv,
    at_y_send, at_y_recv, at_z_send, at_z_recv, own_send, own_recv,
    af_y_send, af_y_recv, af_z_send, af_z_recv,
):
    chunks, genes, _ = prior.shape
    me = lax.axis_index("gene")
    core, y, z = me % 2, (me // 2) % 4, me // 8
    partner = z * 8 + y * 2 + (1 - core)
    across = (1 - z) * 8 + y * 2 + core
    turns = (1, 3, 2)
    ys = [(y + dy) % 4 for dy in turns]

    x_copy = pltpu.make_async_copy(x_hbm, x, x_sem)

    def prior_copy(n):
        columns = pl.ds(pl.multiple_of(n * CHUNK, CHUNK), CHUNK)
        return pltpu.make_async_copy(prior_hbm.at[:, columns], prior.at[n], prior_sem.at[n])

    prior_copy(0).start()
    x_copy.start()
    for n in range(1, chunks):
        prior_copy(n).start()

    def device_of(y_to):
        return z * 8 + y_to * 2 + core

    barrier = pltpu.get_barrier_semaphore()
    for device in [device_of(y_to) for y_to in ys] + [across, partner]:
        pl.semaphore_signal(barrier, inc=1, device_id={"gene": device}, device_id_type=MESH)
    pl.semaphore_wait(barrier, len(ys) + 2)

    for b in range(mask_ref.shape[1]):
        lanes = slice(b % 2 * BLOCK, b % 2 * BLOCK + BLOCK)
        support[b // 2, :, lanes] = jnp.broadcast_to(
            mask_ref[:, b : b + 1].astype(jnp.float32), (support.shape[1], BLOCK)
        )

    def remote(src, dst, send, recv, device):
        return pltpu.make_async_remote_copy(
            src_ref=src, dst_ref=dst, send_sem=send, recv_sem=recv,
            device_id={"gene": device}, device_id_type=MESH,
        )

    def pair_copy(n):
        return remote(
            part.at[n, :, :, 1 - core], pair.at[n], pair_send.at[n], pair_recv.at[n], partner
        )

    def rs_y(n, z_first, y_to, slot):
        if z_first:
            src, dst = mid_z.at[n, y_to], last_z.at[n, slot]
        else:
            src, dst = total.at[n, :, y_to], near_y.at[n, slot]
        return remote(src, dst, rs_y_send.at[n, y_to], rs_y_recv.at[n, slot], device_of(y_to))

    def rs_z(n, z_first):
        if z_first:
            src, dst = total.at[n, 1 - z], near_z.at[n]
        else:
            src, dst = mid_y.at[n, 1 - z], last_y.at[n]
        return remote(src, dst, rs_z_send.at[n], rs_z_recv.at[n], across)

    def ag_y(n, z_first, y_to, slot):
        block = scores.at[n, :, slot, core] if z_first else scores.at[n, z, slot, core]
        return remote(
            block, block, ag_y_send.at[n, y_to], ag_y_recv.at[n, slot], device_of(y_to)
        )

    def ag_z(n, z_first, side):
        block = scores.at[n, side, y, core] if z_first else scores.at[n, side, :, core]
        return remote(block, block, ag_z_send.at[n], ag_z_recv.at[n], across)

    def fw_copy(n, side):
        block = scores.at[n, :, :, side]
        return remote(block, block, fw_send.at[n], fw_recv.at[n], partner)

    def wide(value):
        return value.astype(jnp.float32)

    def by_order(n, parity, step):
        @pl.when(n % 2 == parity)
        def _():
            step(True)

        @pl.when(n % 2 != parity)
        def _():
            step(False)

    def multiply(n):
        prior_copy(n).wait()

        rows = jnp.broadcast_to(support[n][:, None], (support.shape[1], 16, CHUNK))
        masked = prior[n].reshape(-1, BLOCK // 16, 16, CHUNK) * rows.astype(jnp.bfloat16)[:, None]
        prior[n] = masked.reshape(prior.shape[1:])
        product = jnp.dot(x[...], prior[n], preferred_element_type=jnp.float32)
        part[n] = product.astype(jnp.bfloat16).reshape(part.shape[1:])
        pair_copy(n).start()

    def spread(n):
        pair_copy(n).wait_recv()
        total[n] = (wide(part[n, :, :, core]) + wide(pair[n])).astype(jnp.bfloat16)

        def step(z_first):
            if z_first:
                rs_z(n, True).start()
            else:
                for y_to in ys:
                    rs_y(n, False, y_to, y).start()

        by_order(n, 0, step)

    def middle(n):
        def step(z_first):
            if z_first:
                rs_z(n, True).wait_recv()
                mid_z[n] = (wide(total[n, z]) + wide(near_z[n])).astype(jnp.bfloat16)
                for y_to in ys:
                    rs_y(n, True, y_to, y).start()
            else:
                value = wide(total[n, :, y])
                for slot in ys:
                    rs_y(n, False, y, slot).wait_recv()
                    value = value + wide(near_y[n, slot])
                mid_y[n] = value.astype(jnp.bfloat16)
                rs_z(n, False).start()

        by_order(n, 0, step)

    def collect(n):
        def step(z_first):
            if z_first:
                value = wide(mid_z[n, y])
                for slot in ys:
                    rs_y(n, True, y, slot).wait_recv()
                    value = value + wide(last_z[n, slot])
            else:
                rs_z(n, False).wait_recv()
                value = wide(mid_y[n, z]) + wide(last_y[n])
            scores[n, z, y, core] = value.astype(jnp.bfloat16)

        by_order(n, 0, step)

        def out(z_first):
            if z_first:
                ag_z(n, True, z).start()
            else:
                for y_to in ys:
                    ag_y(n, False, y_to, y).start()

        by_order(n, 1, out)

    def relay(n):
        def step(z_first):
            if z_first:
                ag_z(n, True, 1 - z).wait_recv()
                for y_to in ys:
                    ag_y(n, True, y_to, y).start()
            else:
                for slot in ys:
                    ag_y(n, False, y, slot).wait_recv()
                ag_z(n, False, z).start()

        by_order(n, 1, step)

    def share(n):
        def step(z_first):
            if z_first:
                for slot in ys:
                    ag_y(n, True, y, slot).wait_recv()
            else:
                ag_z(n, False, 1 - z).wait_recv()

        by_order(n, 1, step)
        fw_copy(n, core).start()

    acc[...] = jnp.zeros_like(acc)

    def mix(n):
        fw_copy(n, 1 - core).wait_recv()
        lanes = pl.ds(pl.multiple_of(n * CHUNK, CHUNK), CHUNK)
        acc[...] += lax.dot_general(
            gram_ref[:, lanes], scores[n].reshape(-1, CHUNK), (((1,), (1,)), ((), ())),
            preferred_element_type=jnp.float32,
        )

    x_copy.wait()
    stages = (
        (LAGS[0], multiply), (LAGS[1], spread), (LAGS[2], middle), (LAGS[3], collect),
        (LAGS[4], relay), (LAGS[5], share), (LAGS[6], mix),
    )

    def turn(i, carry):
        for lag, stage in stages:
            @pl.when((i >= lag) & (i < lag + chunks))
            def _():
                stage(i - lag)

        return carry

    lax.fori_loop(0, chunks + LAGS[-1], turn, 0)

    at_ref[z, y, core] = acc[...].astype(jnp.bfloat16)
    spread_at = Spread(
        at_ref, (z, y, core), slice(0, SPLIT), slice(SPLIT, at_ref.shape[3]),
        [(y_to, {"gene": device_of(y_to)}) for y_to in ys], {"gene": across}, {"gene": partner},
        (at_y_send, at_y_recv, at_z_send, at_z_recv, own_send, own_recv),
        (af_y_send, af_y_recv, af_z_send, af_z_recv),
    )
    spread_at.begin()
    spread_at.relay_high()
    spread_at.relay_low()
    spread_at.finish()

    def drain(n, carry):
        pair_copy(n).wait_send()
        fw_copy(n, core).wait_send()

        def reduced(z_first):
            rs_z(n, z_first).wait_send()
            for y_to in ys:
                rs_y(n, z_first, y_to, y).wait_send()

        by_order(n, 0, reduced)

        def gathered(z_first):
            ag_z(n, z_first, z).wait_send()
            for y_to in ys:
                ag_y(n, z_first, y_to, y).wait_send()

        by_order(n, 1, gathered)
        return carry

    lax.fori_loop(0, chunks, drain, 0)
    spread_at.drain()


def activity_of(expression, prior_values, block_mask, gram_inverse):
    devices = lax.axis_size("gene")
    cells, genes = expression.shape
    factors = prior_values.shape[1]
    own = gram_inverse.shape[1]
    chunks = factors // CHUNK
    rows = cells // devices
    bf = jnp.bfloat16
    vmem, dma = pltpu.VMEM, pltpu.SemaphoreType.DMA
    blocks = pl.pallas_call(
        activity_kernel,
        out_shape=jax.ShapeDtypeStruct((2, 4, 2, own, cells), bf),
        in_specs=[pl.BlockSpec(memory_space=pl.ANY)] * 2
        + [pl.BlockSpec(memory_space=pltpu.VMEM)] * 2,
        out_specs=pl.BlockSpec(memory_space=pltpu.VMEM),
        scratch_shapes=[
            vmem((cells, genes), bf),
            vmem((chunks, genes, CHUNK), bf),
            vmem((chunks, genes // BLOCK, CHUNK), jnp.float32),
            vmem((chunks, 2, 4, 2, rows, CHUNK), bf),
            vmem((chunks, 2, 4, rows, CHUNK), bf),
            vmem((chunks, 2, 4, rows, CHUNK), bf),
            vmem((chunks, 4, rows, CHUNK), bf),
            vmem((chunks, 4, 2, rows, CHUNK), bf),
            vmem((chunks, 4, rows, CHUNK), bf),
            vmem((chunks, 2, rows, CHUNK), bf),
            vmem((chunks, 4, rows, CHUNK), bf),
            vmem((chunks, rows, CHUNK), bf),
            vmem((chunks, 2, 4, 2, rows, CHUNK), bf),
            vmem((own, cells), jnp.float32),
            dma, dma((chunks,)), dma((chunks,)), dma((chunks,)),
            dma((chunks, 4)), dma((chunks, 4)), dma((chunks,)), dma((chunks,)),
            dma((chunks, 4)), dma((chunks, 4)), dma((chunks,)), dma((chunks,)),
            dma((chunks,)), dma((chunks,)),
            dma((2, 4)), dma((2, 4)), dma((2,)), dma((2,)), dma, dma,
            dma((2, 4)), dma((2, 4)), dma((2,)), dma((2,)),
        ],
        compiler_params=pltpu.CompilerParams(
            collective_id=0, has_side_effects=True, vmem_limit_bytes=56 * 2**20
        ),
        name="activity",
    )(expression, prior_values, block_mask, gram_inverse.T)
    return blocks


Z_ROWS = 768
HOPS = 4


def solve_kernel(
    at_hbm, x_hbm, mask_ref, out_ref,
    at_ref, x, part, z1, zs, r1, x1, r2, x2, xs, z2, gram_part, gram_z, gram_mid, gram_x, gram, squares, penalty,
    first, coef, coef_bf, sent,
    at_sem, x_sem, z1_send, z1_recv, r1_send, r1_recv, x1_send, x1_recv, r2_send, r2_recv,
    x2_send, x2_recv, z2_send, z2_recv,
    gz_send, gz_recv, gx_send, gx_recv, hx_send, hx_recv, hz_send, hz_recv,
    gy_send, gy_recv, ga_send, ga_recv, own_send, own_recv, fy_send, fy_recv, fz_send, fz_recv,
    sq_send, sq_recv, out_send, out_recv,
):
    cells = 2 * HOPS
    pieces = at_ref.shape[3] // 16
    factors, width = first.shape
    cell, gene = lax.axis_index("cell"), lax.axis_index("gene")
    x_at, z_lo = cell % HOPS, cell // HOPS
    core, y_at, z_hi = gene % 2, (gene // 2) % 4, gene // 8
    z_partner = (1 - z_lo) * HOPS + x_at
    core_partner = z_hi * 8 + y_at * 2 + (1 - core)
    right, left, far = [(x_at + dx) % HOPS for dx in (1, 3, 2)]
    xs_at = [right, left, far]
    ys_at = [(y_at + dy) % 4 for dy in (1, 3, 2)]
    across = (z_partner, (1 - z_hi) * 8 + y_at * 2 + core)

    def remote(src, dst, send, recv, at_cell, at_gene):
        return pltpu.make_async_remote_copy(
            src_ref=src, dst_ref=dst, send_sem=send, recv_sem=recv,
            device_id={"cell": at_cell, "gene": at_gene}, device_id_type=MESH,
        )

    tail = x_hbm.shape[1] - (cells - 1) * width

    def x_copy(d):
        lanes = tail if d == cells - 1 else width
        return pltpu.make_async_copy(
            x_hbm.at[:, pl.ds(d * width, lanes)], x.at[d, :, pl.ds(0, lanes)], x_sem.at[d]
        )

    at_copy = pltpu.make_async_copy(at_hbm, at_ref, at_sem)
    at_copy.start()
    for d in range(cells):
        x_copy(d).start()
    x[cells - 1, :, tail:] = jnp.zeros((x.shape[1], width - tail), x.dtype)

    barrier = pltpu.get_barrier_semaphore()
    greeted = [((cell + o) % cells, gene) for o in range(1, cells)]
    greeted += [(cell, z_hi * 8 + y_to * 2 + core) for y_to in ys_at]
    greeted += [across, (cell, core_partner)]
    for at_cell, at_gene in greeted:
        pl.semaphore_signal(
            barrier, inc=1, device_id={"cell": at_cell, "gene": at_gene}, device_id_type=MESH
        )
    pl.semaphore_wait(barrier, len(greeted))

    at_copy.wait()
    whole = at_ref[...].reshape(factors, -1)
    product = lax.dot_general(
        at_ref[z_hi, y_at, core], whole, (((1,), (1,)), ((), ())),
        preferred_element_type=jnp.float32,
    )
    gram_part[:pieces] = product.astype(jnp.bfloat16).reshape(pieces, 16, factors)
    gram_part[pieces:] = jnp.zeros_like(gram_part[pieces:])

    def gz_copy():
        src = gram_part.at[pl.ds((1 - z_lo) * HOPS, HOPS)]
        return remote(src, gram_z, gz_send, gz_recv, z_partner, gene)

    def gx_copy(x_to, slot):
        return remote(
            gram_mid.at[x_to], gram_x.at[slot], gx_send.at[x_to], gx_recv.at[slot],
            z_lo * HOPS + x_to, gene,
        )

    def hx_copy(x_to, slot):
        block = gram.at[z_hi, y_at, core, z_lo * HOPS + slot]
        return remote(
            block, block, hx_send.at[x_to], hx_recv.at[slot], z_lo * HOPS + x_to, gene
        )

    def hz_copy(side):
        block = gram.at[z_hi, y_at, core, pl.ds(side * HOPS, HOPS)]
        return remote(block, block, hz_send, hz_recv, z_partner, gene)

    gz_copy().start()

    for d in range(cells):
        x_copy(d).wait()

    def z1_copy(x_to):
        d = (1 - z_lo) * HOPS + x_to
        return remote(
            part.at[d, pl.ds(0, Z_ROWS)], z1.at[x_to], z1_send.at[x_to], z1_recv.at[x_to],
            z_partner, gene,
        )

    rest = pl.ds(Z_ROWS, factors - Z_ROWS)

    def toward(k):
        return z_lo * HOPS + (left if k else right)

    def r1_copy(k):
        z_to = z_lo if k else 1 - z_lo
        return remote(
            part.at[z_to * HOPS + far, rest], r1.at[k], r1_send.at[k], r1_recv.at[k],
            toward(k), gene,
        )

    def x1_copy(z_to, k):
        return remote(
            part.at[z_to * HOPS + (left if k else right), rest], x1.at[z_to, k],
            x1_send.at[z_to, k], x1_recv.at[z_to, k], toward(k), gene,
        )

    def pass_on(k):
        z_to = z_lo if k else 1 - z_lo
        d = z_to * HOPS + (left if k else right)
        r1_copy(k).wait_recv()
        value = part[d, Z_ROWS:].astype(jnp.float32) + r1[k].astype(jnp.float32)
        part[d, Z_ROWS:] = value.astype(jnp.bfloat16)
        x1_copy(z_to, k).start()

    half = Z_ROWS // 2

    def r2_copy(k):
        return remote(
            zs.at[far, pl.ds(k * half, half)], r2.at[k], r2_send.at[k], r2_recv.at[k],
            toward(k), gene,
        )

    def x2_copy(k):
        return remote(
            zs.at[left if k else right], x2.at[k], x2_send.at[k], x2_recv.at[k], toward(k), gene
        )

    def z2_copy():
        return remote(xs, z2, z2_send, z2_recv, z_partner, gene)

    def order(i):
        return (x_at + 2 - i + (i // 2) * (2 * i - 1)) % HOPS

    def multiply(i, carry):
        x_to = order(i % HOPS)
        z_to = (z_lo + 1 + i // HOPS) % 2
        d = z_to * HOPS + x_to
        value = jnp.dot(
            at_ref[...].reshape(factors, -1), x[d], preferred_element_type=jnp.float32
        )
        part[d] = value.astype(jnp.bfloat16)

        @pl.when(i < 2)
        def _():
            z1_copy(x_to).start()

        @pl.when(i == 0)
        def _():
            r1_copy(0).start()

        @pl.when(i == 2)
        def _():
            x1_copy(1 - z_lo, 1).start()

        return carry

    lax.fori_loop(0, HOPS, multiply, 0)

    gz_copy().wait_recv()
    mine = gram_part[pl.ds(z_lo * HOPS, HOPS)].astype(jnp.float32)
    gram_mid[...] = (mine + gram_z[...].astype(jnp.float32)).astype(jnp.bfloat16)
    for x_to in xs_at:
        gx_copy(x_to, x_at).start()

    lax.fori_loop(HOPS, cells, multiply, 0)

    def sq_copy(t, slot):
        return remote(squares.at[slot], squares.at[slot], sq_send.at[t], sq_recv.at[slot], t, gene)

    def square(b, total):
        value = at_ref[b // 8, b // 2 % 4, b % 2].astype(jnp.float32)
        return total + jnp.sum((value * value).reshape(-1, 8, value.shape[1]), axis=0)

    squares[cell] = lax.fori_loop(
        0, 16, square, jnp.zeros(squares.shape[1:], jnp.float32)
    )
    for o in range(1, cells):
        sq_copy((cell + o) % cells, cell).start()

    for h in range(width // BLOCK):
        gene_block = 2 * cell + h * (1 - cell // (cells - 1))
        relief = mask_ref[pl.ds(gene_block, 1)].astype(jnp.float32)
        row = LASSO * (1.0 - PRIOR_RELIEF * relief)
        for b in range(mask_ref.shape[1]):
            block = jnp.broadcast_to(row[:, b : b + 1], (BLOCK, BLOCK))
            penalty[b * BLOCK : (b + 1) * BLOCK, h * BLOCK : (h + 1) * BLOCK] = block

    def pair_sum(i):
        x_to = order(i)
        z1_copy(x_to).wait_recv()
        own = part[z_lo * HOPS + x_to, :Z_ROWS].astype(jnp.float32)
        value = own + z1[x_to].astype(jnp.float32)
        zs[x_to] = value.astype(jnp.bfloat16)
        if i == 0:
            r2_copy(0).start()
            r2_copy(1).start()
        elif i < HOPS - 1:
            k = i - 1
            rows = pl.ds(k * half, half)
            r2_copy(k).wait_recv()
            value = zs[x_to, rows].astype(jnp.float32) + r2[k].astype(jnp.float32)
            zs[x_to, rows] = value.astype(jnp.bfloat16)
            x2_copy(k).start()

    value = gram_mid[x_at].astype(jnp.float32)
    for slot in xs_at:
        gx_copy(x_at, slot).wait_recv()
        value = value + gram_x[slot].astype(jnp.float32)
    gram[z_hi, y_at, core, cell] = value.astype(jnp.bfloat16)
    for x_to in xs_at:
        hx_copy(x_to, x_at).start()
    r1_copy(1).start()
    pass_on(0)
    pair_sum(0)
    x1_copy(z_lo, 0).start()

    for slot in xs_at:
        hx_copy(x_at, slot).wait_recv()
    hz_copy(z_lo).start()
    for i in range(2, HOPS):
        z1_copy(order(i)).start()

    hz_copy(1 - z_lo).wait_recv()
    spread = Spread(
        gram, (z_hi, y_at, core), slice(0, HOPS), slice(HOPS, pieces),
        [(y_to, {"cell": cell, "gene": z_hi * 8 + y_to * 2 + core}) for y_to in ys_at],
        {"cell": across[0], "gene": across[1]}, {"cell": cell, "gene": core_partner},
        (gy_send, gy_recv, ga_send, ga_recv, own_send, own_recv),
        (fy_send, fy_recv, fz_send, fz_recv),
    )
    spread.begin()
    pass_on(1)
    spread.relay_high()
    pair_sum(1)
    pair_sum(2)

    value = part[(1 - z_lo) * HOPS + x_at, Z_ROWS:].astype(jnp.float32)
    for k in range(2):
        x1_copy(1 - z_lo, k).wait_recv()
        value = value + x1[1 - z_lo, k].astype(jnp.float32)
    xs[...] = value.astype(jnp.bfloat16)
    z2_copy().start()
    spread.relay_low()
    pair_sum(3)

    for o in range(1, cells):
        sq_copy(cell, (cell + o) % cells).wait_recv()
    sum_squares = jnp.sum(jnp.sum(squares[...], axis=0), keepdims=True)
    total_cells = cells * x.shape[1]
    step_size = 0.5 / (sum_squares / (total_cells * factors) + EPSILON)
    scale = step_size / total_cells
    inverse = 1.0 / (1.0 + step_size * RIDGE)

    def shrunk(moved, rows):
        limit = step_size * penalty[rows]
        return (jnp.maximum(moved - limit, 0.0) - jnp.maximum(-moved - limit, 0.0)) * inverse

    def start_from(value, rows):
        first[rows] = value
        start = shrunk(scale * value, rows)
        coef[rows] = start
        coef_bf[rows] = start.astype(jnp.bfloat16)

    for k in range(2):
        x2_copy(k).wait_recv()
        x1_copy(z_lo, k).wait_recv()

    def z_block(b, carry):
        rows = pl.ds(pl.multiple_of(b * BLOCK, BLOCK), BLOCK)
        value = zs[x_at, rows].astype(jnp.float32)
        for k in range(2):
            value = value + x2[k, rows].astype(jnp.float32)
        start_from(value, rows)
        return carry

    lax.fori_loop(0, Z_ROWS // BLOCK, z_block, 0)
    z2_copy().wait_recv()

    def x_block(b, carry):
        low = pl.ds(pl.multiple_of(b * BLOCK, BLOCK), BLOCK)
        rows = pl.ds(pl.multiple_of(b * BLOCK + Z_ROWS, BLOCK), BLOCK)
        value = part[cell, rows].astype(jnp.float32) + z2[low].astype(jnp.float32)
        for k in range(2):
            value = value + x1[z_lo, k, low].astype(jnp.float32)
        start_from(value, rows)
        return carry

    lax.fori_loop(0, (factors - Z_ROWS) // BLOCK, x_block, 0)

    spread.finish()
    height = out_ref.shape[0]

    def out_copy(t, slot):
        lanes = pl.ds(pl.multiple_of(slot * width, width), width)
        return remote(sent.at[t], out_ref.at[:, lanes], out_send.at[t], out_recv.at[slot], t, gene)

    def finish(i, carry):
        p = (cell // 2 + 1 + i) % HOPS
        rows = pl.ds(pl.multiple_of(p * (2 * height), 64), 2 * height)
        block = gram[p // 2, pl.ds(p % 2 * 2, 2), :, :pieces].reshape(2 * height, factors)
        second = jnp.dot(block, coef_bf[...], preferred_element_type=jnp.float32)
        moved = coef[rows] - scale * (second - first[rows])
        value = (shrunk(moved, rows) * OUT_UNITS).astype(jnp.bfloat16)
        for h in range(2):
            t = 2 * p + h
            piece = value[h * height : (h + 1) * height]

            @pl.when(t != cell)
            def _():
                sent[t] = piece
                out_copy(t, cell).start()

            @pl.when(t == cell)
            def _():
                out_ref[:, pl.ds(pl.multiple_of(cell * width, width), width)] = piece

        return carry

    lax.fori_loop(0, HOPS, finish, 0)

    gz_copy().wait_send()
    hz_copy(z_lo).wait_send()
    for x_to in xs_at:
        gx_copy(x_to, x_at).wait_send()
        hx_copy(x_to, x_at).wait_send()
    spread.drain()

    for x_to in range(HOPS):
        z1_copy(x_to).wait_send()
    for k in range(2):
        r1_copy(k).wait_send()
        r2_copy(k).wait_send()
        x2_copy(k).wait_send()
        for z_to in range(2):
            x1_copy(z_to, k).wait_send()
    z2_copy().wait_send()
    for o in range(1, cells):
        t = (cell + o) % cells
        sq_copy(t, cell).wait_send()
        out_copy(t, cell).wait_send()
        out_copy(cell, t).wait_recv()


def solve(activity_t, expression, block_mask):
    cell_devices, gene_devices = lax.axis_size("cell"), lax.axis_size("gene")
    own, cells = activity_t.shape[-2:]
    factors = gene_devices * own
    width = CHUNK
    rest = factors - Z_ROWS
    bf, f32 = jnp.bfloat16, jnp.float32
    vmem, dma = pltpu.VMEM, pltpu.SemaphoreType.DMA
    return pl.pallas_call(
        solve_kernel,
        out_shape=jax.ShapeDtypeStruct((factors // cell_devices, cell_devices * width), bf),
        in_specs=[
            pl.BlockSpec(memory_space=pl.ANY),
            pl.BlockSpec(memory_space=pl.ANY),
            pl.BlockSpec(memory_space=pltpu.VMEM),
        ],
        out_specs=pl.BlockSpec(memory_space=pltpu.VMEM),
        scratch_shapes=[
            vmem(activity_t.shape, bf),
            vmem((cell_devices, cells, width), bf),
            vmem((cell_devices, factors, width), bf),
            vmem((HOPS, Z_ROWS, width), bf),
            vmem((HOPS, Z_ROWS, width), bf),
            vmem((2, rest, width), bf),
            vmem((2, 2, rest, width), bf),
            vmem((2, Z_ROWS // 2, width), bf),
            vmem((2, Z_ROWS, width), bf),
            vmem((rest, width), bf),
            vmem((rest, width), bf),
            vmem((cell_devices, 16, factors), bf),
            vmem((HOPS, 16, factors), bf),
            vmem((HOPS, 16, factors), bf),
            vmem((HOPS, 16, factors), bf),
            vmem((2, 4, 2, cell_devices, 16, factors), bf),
            vmem((cell_devices, 8, cells), f32),
            vmem((factors, width), f32),
            vmem((factors, width), f32),
            vmem((factors, width), f32),
            vmem((factors, width), bf),
            vmem((cell_devices, factors // cell_devices, width), bf),
            dma, dma((cell_devices,)),
            dma((HOPS,)), dma((HOPS,)),
            dma((2,)), dma((2,)), dma((2, 2)), dma((2, 2)),
            dma((2,)), dma((2,)), dma((2,)), dma((2,)),
            dma, dma,
            dma, dma, dma((HOPS,)), dma((HOPS,)), dma((HOPS,)), dma((HOPS,)), dma, dma,
            dma((2, 4)), dma((2, 4)), dma((2,)), dma((2,)), dma, dma,
            dma((2, 4)), dma((2, 4)), dma((2,)), dma((2,)),
            dma((cell_devices,)), dma((cell_devices,)),
            dma((cell_devices,)), dma((cell_devices,)),
        ],
        compiler_params=pltpu.CompilerParams(
            collective_id=1, has_side_effects=True, vmem_limit_bytes=60 * 2**20
        ),
        name="solve",
    )(activity_t, expression, block_mask)


def on_device(expression, prior_values, block_mask, gram_inverse):
    activity_t = activity_of(expression, prior_values, block_mask, gram_inverse)
    rows = solve(activity_t, expression, block_mask)
    return rows[:, : expression.shape[1]].astype(jnp.float32)


def solution(mesh):
    in_specs = (P("cell", "gene"), P("gene", None), P("gene", None), P(None, "gene"))
    out_specs = P("cell", "gene")
    return jax.shard_map(
        on_device, mesh=mesh, in_specs=in_specs, out_specs=out_specs, check_vma=False
    )
```

```python
import functools

import jax
import jax.numpy as jnp
from jax import lax
from jax.experimental import pallas as pl
from jax.experimental.pallas import tpu as pltpu
from jax.sharding import PartitionSpec as P

BLOCK = 128

OUT_UNITS = 100.0
LASSO = 0.006
RIDGE = 0.1
PRIOR_RELIEF = 0.7
EPSILON = 1e-06

MESH = pl.DeviceIdType.MESH
CHUNK = 256
CUTS = (32, 80)
SPLIT = 48
LAGS = (0, 1, 5, 8, 12, 16, 17)


class Spread:
    def __init__(self, ref, at, low, high, ys, across, partner, direct, handed):
        self.ref, (self.z, self.y, self.core) = ref, at
        self.rows = (low, high)
        self.ys, self.across, self.partner = ys, across, partner
        self.y_send, self.y_recv, self.z_send, self.z_recv, self.own_send, self.own_recv = direct
        self.fy_send, self.fy_recv, self.fz_send, self.fz_recv = handed

    def remote(self, block, send, recv, device):
        return pltpu.make_async_remote_copy(
            src_ref=block, dst_ref=block, send_sem=send, recv_sem=recv,
            device_id=device, device_id_type=MESH,
        )

    def own(self, side):
        block = self.ref.at[self.z, self.y, side]
        return self.remote(block, self.own_send, self.own_recv, self.partner)

    def over_y(self, k, device, y_to, slot):
        zs = slice(None) if k else self.z
        block = self.ref.at[zs, slot, self.core, self.rows[k]]
        return self.remote(block, self.y_send.at[k, y_to], self.y_recv.at[k, slot], device)

    def over_z(self, k, side):
        ys = self.y if k else slice(None)
        block = self.ref.at[side, ys, self.core, self.rows[k]]
        return self.remote(block, self.z_send.at[k], self.z_recv.at[k], self.across)

    def hand_y(self, k, slot, side):
        zs = slice(None) if k else self.z
        block = self.ref.at[zs, slot, side, self.rows[k]]
        return self.remote(block, self.fy_send.at[k, slot], self.fy_recv.at[k, slot], self.partner)

    def hand_z(self, k, side):
        ys = self.y if k else slice(None)
        block = self.ref.at[1 - self.z, ys, side, self.rows[k]]
        return self.remote(block, self.fz_send.at[k], self.fz_recv.at[k], self.partner)

    def begin(self):
        self.over_z(1, self.z).start()
        for y_to, device in self.ys:
            self.over_y(0, device, y_to, self.y).start()
        self.own(self.core).start()

    def relay_high(self):
        self.over_z(1, 1 - self.z).wait_recv()
        for y_to, device in self.ys:
            self.over_y(1, device, y_to, self.y).start()
        self.hand_z(1, self.core).start()

    def relay_low(self):
        for slot, device in self.ys:
            self.over_y(0, device, self.y, slot).wait_recv()
        self.over_z(0, self.z).start()
        for slot, _ in self.ys:
            self.hand_y(0, slot, self.core).start()

    def finish(self):
        for slot, device in self.ys:
            self.over_y(1, device, self.y, slot).wait_recv()
            self.hand_y(1, slot, self.core).start()
        self.over_z(0, 1 - self.z).wait_recv()
        self.hand_z(0, self.core).start()
        self.own(1 - self.core).wait_recv()
        for k in range(2):
            self.hand_z(k, 1 - self.core).wait_recv()
            for slot, _ in self.ys:
                self.hand_y(k, slot, 1 - self.core).wait_recv()

    def drain(self):
        self.own(self.core).wait_send()
        for k in range(2):
            self.over_z(k, self.z).wait_send()
            self.hand_z(k, self.core).wait_send()
            for y_to, device in self.ys:
                self.over_y(k, device, y_to, self.y).wait_send()
                self.hand_y(k, y_to, self.core).wait_send()


class RelaySpread(Spread):
    def relayed_by(self, cuts, send, recv):
        self.near, self.far = self.ys[:2], self.ys[2][0]
        self.halves = [(slice(r.start, c), slice(c, r.stop)) for r, c in zip(self.rows, cuts)]
        self.w_send, self.w_recv = send, recv

    def onward(self, k, j, slot):
        zs = slice(None) if k else self.z
        block = self.ref.at[zs, slot, self.core, self.halves[k][j]]
        return self.remote(block, self.w_send.at[k, j], self.w_recv.at[k, j], self.near[j][1])

    def forward(self, k):
        for j in range(2):
            slot, device = self.near[1 - j]
            self.over_y(k, device, self.y, slot).wait_recv()
            self.onward(k, j, slot).start()
            self.hand_y(k, slot, self.core).start()

    def from_far(self, k):
        for j in range(2):
            self.onward(k, j, self.far).wait_recv()
        self.hand_y(k, self.far, self.core).start()

    def run(self):
        self.over_z(1, self.z).start()
        for y_to, device in self.near:
            self.over_y(0, device, y_to, self.y).start()
        self.own(self.core).start()
        self.forward(0)
        self.over_z(1, 1 - self.z).wait_recv()
        for y_to, device in self.near:
            self.over_y(1, device, y_to, self.y).start()
        self.hand_z(1, self.core).start()
        self.from_far(0)
        self.over_z(0, self.z).start()
        self.forward(1)
        self.from_far(1)
        self.over_z(0, 1 - self.z).wait_recv()
        self.hand_z(0, self.core).start()
        self.own(1 - self.core).wait_recv()
        for k in range(2):
            self.hand_z(k, 1 - self.core).wait_recv()
            for slot, _ in self.ys:
                self.hand_y(k, slot, 1 - self.core).wait_recv()

    def drain(self):
        self.own(self.core).wait_send()
        for k in range(2):
            self.over_z(k, self.z).wait_send()
            self.hand_z(k, self.core).wait_send()
            for y_to, device in self.near:
                self.over_y(k, device, y_to, self.y).wait_send()
            for j in range(2):
                self.onward(k, j, self.near[1 - j][0]).wait_send()
            for y_to, _ in self.ys:
                self.hand_y(k, y_to, self.core).wait_send()


def activity_kernel(
    x_hbm, prior_hbm, mask_ref, gram_ref, at_ref,
    x, prior, support, part, pair, total, near_z, near_y, mid_z, mid_y, last_z, last_y, scores, acc,
    x_sem, prior_sem, pair_send, pair_recv,
    rs_y_send, rs_y_recv, rs_z_send, rs_z_recv,
    ag_y_send, ag_y_recv, ag_z_send, ag_z_recv, fw_send, fw_recv,
    at_y_send, at_y_recv, at_z_send, at_z_recv, own_send, own_recv,
    af_y_send, af_y_recv, af_z_send, af_z_recv, af_w_send, af_w_recv,
):
    chunks, genes, _ = prior.shape
    me = lax.axis_index("gene")
    core, y, z = me % 2, (me // 2) % 4, me // 8
    partner = z * 8 + y * 2 + (1 - core)
    across = (1 - z) * 8 + y * 2 + core
    turns = (1, 3, 2)
    ys = [(y + dy) % 4 for dy in turns]

    x_copy = pltpu.make_async_copy(x_hbm, x, x_sem)

    def prior_copy(n):
        columns = pl.ds(pl.multiple_of(n * CHUNK, CHUNK), CHUNK)
        return pltpu.make_async_copy(prior_hbm.at[:, columns], prior.at[n], prior_sem.at[n])

    prior_copy(0).start()
    x_copy.start()
    for n in range(1, chunks):
        prior_copy(n).start()

    def device_of(y_to):
        return z * 8 + y_to * 2 + core

    barrier = pltpu.get_barrier_semaphore()
    for device in [device_of(y_to) for y_to in ys] + [across, partner]:
        pl.semaphore_signal(barrier, inc=1, device_id={"gene": device}, device_id_type=MESH)
    pl.semaphore_wait(barrier, len(ys) + 2)

    for b in range(mask_ref.shape[1]):
        lanes = slice(b % 2 * BLOCK, b % 2 * BLOCK + BLOCK)
        support[b // 2, :, lanes] = jnp.broadcast_to(
            mask_ref[:, b : b + 1].astype(jnp.float32), (support.shape[1], BLOCK)
        )

    def remote(src, dst, send, recv, device):
        return pltpu.make_async_remote_copy(
            src_ref=src, dst_ref=dst, send_sem=send, recv_sem=recv,
            device_id={"gene": device}, device_id_type=MESH,
        )

    def pair_copy(n):
        return remote(
            part.at[n, :, :, 1 - core], pair.at[n], pair_send.at[n], pair_recv.at[n], partner
        )

    def rs_y(n, z_first, y_to, slot):
        if z_first:
            src, dst = mid_z.at[n, y_to], last_z.at[n, slot]
        else:
            src, dst = total.at[n, :, y_to], near_y.at[n, slot]
        return remote(src, dst, rs_y_send.at[n, y_to], rs_y_recv.at[n, slot], device_of(y_to))

    def rs_z(n, z_first):
        if z_first:
            src, dst = total.at[n, 1 - z], near_z.at[n]
        else:
            src, dst = mid_y.at[n, 1 - z], last_y.at[n]
        return remote(src, dst, rs_z_send.at[n], rs_z_recv.at[n], across)

    def ag_y(n, z_first, y_to, slot):
        block = scores.at[n, :, slot, core] if z_first else scores.at[n, z, slot, core]
        return remote(
            block, block, ag_y_send.at[n, y_to], ag_y_recv.at[n, slot], device_of(y_to)
        )

    def ag_z(n, z_first, side):
        block = scores.at[n, side, y, core] if z_first else scores.at[n, side, :, core]
        return remote(block, block, ag_z_send.at[n], ag_z_recv.at[n], across)

    def fw_copy(n, side):
        block = scores.at[n, :, :, side]
        return remote(block, block, fw_send.at[n], fw_recv.at[n], partner)

    def wide(value):
        return value.astype(jnp.float32)

    def by_order(n, parity, step):
        @pl.when(n % 2 == parity)
        def _():
            step(True)

        @pl.when(n % 2 != parity)
        def _():
            step(False)

    def multiply(n):
        prior_copy(n).wait()

        rows = jnp.broadcast_to(support[n][:, None], (support.shape[1], 16, CHUNK))
        masked = prior[n].reshape(-1, BLOCK // 16, 16, CHUNK) * rows.astype(jnp.bfloat16)[:, None]
        prior[n] = masked.reshape(prior.shape[1:])
        product = jnp.dot(x[...], prior[n], preferred_element_type=jnp.float32)
        part[n] = product.astype(jnp.bfloat16).reshape(part.shape[1:])
        pair_copy(n).start()

    def spread(n):
        pair_copy(n).wait_recv()
        total[n] = (wide(part[n, :, :, core]) + wide(pair[n])).astype(jnp.bfloat16)

        def step(z_first):
            if z_first:
                rs_z(n, True).start()
            else:
                for y_to in ys:
                    rs_y(n, False, y_to, y).start()

        by_order(n, 0, step)

    def middle(n):
        def step(z_first):
            if z_first:
                rs_z(n, True).wait_recv()
                mid_z[n] = (wide(total[n, z]) + wide(near_z[n])).astype(jnp.bfloat16)
                for y_to in ys:
                    rs_y(n, True, y_to, y).start()
            else:
                value = wide(total[n, :, y])
                for slot in ys:
                    rs_y(n, False, y, slot).wait_recv()
                    value = value + wide(near_y[n, slot])
                mid_y[n] = value.astype(jnp.bfloat16)
                rs_z(n, False).start()

        by_order(n, 0, step)

    def collect(n):
        def step(z_first):
            if z_first:
                value = wide(mid_z[n, y])
                for slot in ys:
                    rs_y(n, True, y, slot).wait_recv()
                    value = value + wide(last_z[n, slot])
            else:
                rs_z(n, False).wait_recv()
                value = wide(mid_y[n, z]) + wide(last_y[n])
            scores[n, z, y, core] = value.astype(jnp.bfloat16)

        by_order(n, 0, step)

        def out(z_first):
            if z_first:
                ag_z(n, True, z).start()
            else:
                for y_to in ys:
                    ag_y(n, False, y_to, y).start()

        by_order(n, 1, out)

    def relay(n):
        def step(z_first):
            if z_first:
                ag_z(n, True, 1 - z).wait_recv()
                for y_to in ys:
                    ag_y(n, True, y_to, y).start()
            else:
                for slot in ys:
                    ag_y(n, False, y, slot).wait_recv()
                ag_z(n, False, z).start()

        by_order(n, 1, step)

    def share(n):
        def step(z_first):
            if z_first:
                for slot in ys:
                    ag_y(n, True, y, slot).wait_recv()
            else:
                ag_z(n, False, 1 - z).wait_recv()

        by_order(n, 1, step)
        fw_copy(n, core).start()

    acc[...] = jnp.zeros_like(acc)

    def mix(n):
        fw_copy(n, 1 - core).wait_recv()
        lanes = pl.ds(pl.multiple_of(n * CHUNK, CHUNK), CHUNK)
        acc[...] += lax.dot_general(
            gram_ref[:, lanes], scores[n].reshape(-1, CHUNK), (((1,), (1,)), ((), ())),
            preferred_element_type=jnp.float32,
        )

    x_copy.wait()
    stages = (
        (LAGS[0], multiply), (LAGS[1], spread), (LAGS[2], middle), (LAGS[3], collect),
        (LAGS[4], relay), (LAGS[5], share), (LAGS[6], mix),
    )

    def turn(i, carry):
        for lag, stage in stages:
            @pl.when((i >= lag) & (i < lag + chunks))
            def _():
                stage(i - lag)

        return carry

    lax.fori_loop(0, chunks + LAGS[-1], turn, 0)

    at_ref[z, y, core] = acc[...].astype(jnp.bfloat16)
    spread_at = RelaySpread(
        at_ref, (z, y, core), slice(0, SPLIT), slice(SPLIT, at_ref.shape[3]),
        [(y_to, {"gene": device_of(y_to)}) for y_to in ys], {"gene": across}, {"gene": partner},
        (at_y_send, at_y_recv, at_z_send, at_z_recv, own_send, own_recv),
        (af_y_send, af_y_recv, af_z_send, af_z_recv),
    )
    spread_at.relayed_by(CUTS, af_w_send, af_w_recv)
    spread_at.run()

    def drain(n, carry):
        pair_copy(n).wait_send()
        fw_copy(n, core).wait_send()

        def reduced(z_first):
            rs_z(n, z_first).wait_send()
            for y_to in ys:
                rs_y(n, z_first, y_to, y).wait_send()

        by_order(n, 0, reduced)

        def gathered(z_first):
            ag_z(n, z_first, z).wait_send()
            for y_to in ys:
                ag_y(n, z_first, y_to, y).wait_send()

        by_order(n, 1, gathered)
        return carry

    lax.fori_loop(0, chunks, drain, 0)
    spread_at.drain()


def activity_of(expression, prior_values, block_mask, gram_inverse):
    devices = lax.axis_size("gene")
    cells, genes = expression.shape
    factors = prior_values.shape[1]
    own = gram_inverse.shape[1]
    chunks = factors // CHUNK
    rows = cells // devices
    bf = jnp.bfloat16
    vmem, dma = pltpu.VMEM, pltpu.SemaphoreType.DMA
    blocks = pl.pallas_call(
        activity_kernel,
        out_shape=jax.ShapeDtypeStruct((2, 4, 2, own, cells), bf),
        in_specs=[pl.BlockSpec(memory_space=pl.ANY)] * 2
        + [pl.BlockSpec(memory_space=pltpu.VMEM)] * 2,
        out_specs=pl.BlockSpec(memory_space=pltpu.VMEM),
        scratch_shapes=[
            vmem((cells, genes), bf),
            vmem((chunks, genes, CHUNK), bf),
            vmem((chunks, genes // BLOCK, CHUNK), jnp.float32),
            vmem((chunks, 2, 4, 2, rows, CHUNK), bf),
            vmem((chunks, 2, 4, rows, CHUNK), bf),
            vmem((chunks, 2, 4, rows, CHUNK), bf),
            vmem((chunks, 4, rows, CHUNK), bf),
            vmem((chunks, 4, 2, rows, CHUNK), bf),
            vmem((chunks, 4, rows, CHUNK), bf),
            vmem((chunks, 2, rows, CHUNK), bf),
            vmem((chunks, 4, rows, CHUNK), bf),
            vmem((chunks, rows, CHUNK), bf),
            vmem((chunks, 2, 4, 2, rows, CHUNK), bf),
            vmem((own, cells), jnp.float32),
            dma, dma((chunks,)), dma((chunks,)), dma((chunks,)),
            dma((chunks, 4)), dma((chunks, 4)), dma((chunks,)), dma((chunks,)),
            dma((chunks, 4)), dma((chunks, 4)), dma((chunks,)), dma((chunks,)),
            dma((chunks,)), dma((chunks,)),
            dma((2, 4)), dma((2, 4)), dma((2,)), dma((2,)), dma, dma,
            dma((2, 4)), dma((2, 4)), dma((2,)), dma((2,)), dma((2, 2)), dma((2, 2)),
        ],
        compiler_params=pltpu.CompilerParams(
            collective_id=0, has_side_effects=True, vmem_limit_bytes=56 * 2**20
        ),
        name="activity",
    )(expression, prior_values, block_mask, gram_inverse.T)
    return blocks


Z_ROWS = 768
HOPS = 4


def solve_kernel(
    at_hbm, x_hbm, mask_ref, out_ref,
    at_ref, x, part, z1, zs, r1, x1, r2, x2, xs, z2, gram_part, gram_z, gram_mid, gram_x, gram, squares, penalty,
    first, coef, coef_bf, sent,
    at_sem, x_sem, z1_send, z1_recv, r1_send, r1_recv, x1_send, x1_recv, r2_send, r2_recv,
    x2_send, x2_recv, z2_send, z2_recv,
    gz_send, gz_recv, gx_send, gx_recv, hx_send, hx_recv, hz_send, hz_recv,
    gy_send, gy_recv, ga_send, ga_recv, own_send, own_recv, fy_send, fy_recv, fz_send, fz_recv,
    sq_send, sq_recv, out_send, out_recv,
):
    cells = 2 * HOPS
    pieces = at_ref.shape[3] // 16
    factors, width = first.shape
    cell, gene = lax.axis_index("cell"), lax.axis_index("gene")
    x_at, z_lo = cell % HOPS, cell // HOPS
    core, y_at, z_hi = gene % 2, (gene // 2) % 4, gene // 8
    z_partner = (1 - z_lo) * HOPS + x_at
    core_partner = z_hi * 8 + y_at * 2 + (1 - core)
    right, left, far = [(x_at + dx) % HOPS for dx in (1, 3, 2)]
    xs_at = [right, left, far]
    ys_at = [(y_at + dy) % 4 for dy in (1, 3, 2)]
    across = (z_partner, (1 - z_hi) * 8 + y_at * 2 + core)

    def remote(src, dst, send, recv, at_cell, at_gene):
        return pltpu.make_async_remote_copy(
            src_ref=src, dst_ref=dst, send_sem=send, recv_sem=recv,
            device_id={"cell": at_cell, "gene": at_gene}, device_id_type=MESH,
        )

    tail = x_hbm.shape[1] - (cells - 1) * width

    def x_copy(d):
        lanes = tail if d == cells - 1 else width
        return pltpu.make_async_copy(
            x_hbm.at[:, pl.ds(d * width, lanes)], x.at[d, :, pl.ds(0, lanes)], x_sem.at[d]
        )

    at_copy = pltpu.make_async_copy(at_hbm, at_ref, at_sem)
    at_copy.start()
    for d in range(cells):
        x_copy(d).start()
    x[cells - 1, :, tail:] = jnp.zeros((x.shape[1], width - tail), x.dtype)

    barrier = pltpu.get_barrier_semaphore()
    greeted = [((cell + o) % cells, gene) for o in range(1, cells)]
    greeted += [(cell, z_hi * 8 + y_to * 2 + core) for y_to in ys_at]
    greeted += [across, (cell, core_partner)]
    for at_cell, at_gene in greeted:
        pl.semaphore_signal(
            barrier, inc=1, device_id={"cell": at_cell, "gene": at_gene}, device_id_type=MESH
        )
    pl.semaphore_wait(barrier, len(greeted))

    at_copy.wait()
    whole = at_ref[...].reshape(factors, -1)
    product = lax.dot_general(
        at_ref[z_hi, y_at, core], whole, (((1,), (1,)), ((), ())),
        preferred_element_type=jnp.float32,
    )
    gram_part[:pieces] = product.astype(jnp.bfloat16).reshape(pieces, 16, factors)
    gram_part[pieces:] = jnp.zeros_like(gram_part[pieces:])

    def gz_copy():
        src = gram_part.at[pl.ds((1 - z_lo) * HOPS, HOPS)]
        return remote(src, gram_z, gz_send, gz_recv, z_partner, gene)

    def gx_copy(x_to, slot):
        return remote(
            gram_mid.at[x_to], gram_x.at[slot], gx_send.at[x_to], gx_recv.at[slot],
            z_lo * HOPS + x_to, gene,
        )

    def hx_copy(x_to, slot):
        block = gram.at[z_hi, y_at, core, z_lo * HOPS + slot]
        return remote(
            block, block, hx_send.at[x_to], hx_recv.at[slot], z_lo * HOPS + x_to, gene
        )

    def hz_copy(side):
        block = gram.at[z_hi, y_at, core, pl.ds(side * HOPS, HOPS)]
        return remote(block, block, hz_send, hz_recv, z_partner, gene)

    gz_copy().start()

    for d in range(cells):
        x_copy(d).wait()

    def z1_copy(x_to):
        d = (1 - z_lo) * HOPS + x_to
        return remote(
            part.at[d, pl.ds(0, Z_ROWS)], z1.at[x_to], z1_send.at[x_to], z1_recv.at[x_to],
            z_partner, gene,
        )

    rest = pl.ds(Z_ROWS, factors - Z_ROWS)

    def toward(k):
        return z_lo * HOPS + (left if k else right)

    def r1_copy(k):
        z_to = z_lo if k else 1 - z_lo
        return remote(
            part.at[z_to * HOPS + far, rest], r1.at[k], r1_send.at[k], r1_recv.at[k],
            toward(k), gene,
        )

    def x1_copy(z_to, k):
        return remote(
            part.at[z_to * HOPS + (left if k else right), rest], x1.at[z_to, k],
            x1_send.at[z_to, k], x1_recv.at[z_to, k], toward(k), gene,
        )

    def pass_on(k):
        z_to = z_lo if k else 1 - z_lo
        d = z_to * HOPS + (left if k else right)
        r1_copy(k).wait_recv()
        value = part[d, Z_ROWS:].astype(jnp.float32) + r1[k].astype(jnp.float32)
        part[d, Z_ROWS:] = value.astype(jnp.bfloat16)
        x1_copy(z_to, k).start()

    half = Z_ROWS // 2

    def r2_copy(k):
        return remote(
            zs.at[far, pl.ds(k * half, half)], r2.at[k], r2_send.at[k], r2_recv.at[k],
            toward(k), gene,
        )

    def x2_copy(k):
        return remote(
            zs.at[left if k else right], x2.at[k], x2_send.at[k], x2_recv.at[k], toward(k), gene
        )

    def z2_copy():
        return remote(xs, z2, z2_send, z2_recv, z_partner, gene)

    def order(i):
        return (x_at + 2 - i + (i // 2) * (2 * i - 1)) % HOPS

    def multiply(i, carry):
        x_to = order(i % HOPS)
        z_to = (z_lo + 1 + i // HOPS) % 2
        d = z_to * HOPS + x_to
        value = jnp.dot(
            at_ref[...].reshape(factors, -1), x[d], preferred_element_type=jnp.float32
        )
        part[d] = value.astype(jnp.bfloat16)

        @pl.when(i < 2)
        def _():
            z1_copy(x_to).start()

        @pl.when(i == 0)
        def _():
            r1_copy(0).start()

        @pl.when(i == 2)
        def _():
            x1_copy(1 - z_lo, 1).start()

        return carry

    lax.fori_loop(0, HOPS, multiply, 0)

    gz_copy().wait_recv()
    mine = gram_part[pl.ds(z_lo * HOPS, HOPS)].astype(jnp.float32)
    gram_mid[...] = (mine + gram_z[...].astype(jnp.float32)).astype(jnp.bfloat16)
    for x_to in xs_at:
        gx_copy(x_to, x_at).start()

    lax.fori_loop(HOPS, cells, multiply, 0)

    def sq_copy(t, slot):
        return remote(squares.at[slot], squares.at[slot], sq_send.at[t], sq_recv.at[slot], t, gene)

    def square(b, total):
        value = at_ref[b // 8, b // 2 % 4, b % 2].astype(jnp.float32)
        return total + jnp.sum((value * value).reshape(-1, 8, value.shape[1]), axis=0)

    squares[cell] = lax.fori_loop(
        0, 16, square, jnp.zeros(squares.shape[1:], jnp.float32)
    )
    for o in range(1, cells):
        sq_copy((cell + o) % cells, cell).start()

    for h in range(width // BLOCK):
        gene_block = 2 * cell + h * (1 - cell // (cells - 1))
        relief = mask_ref[pl.ds(gene_block, 1)].astype(jnp.float32)
        row = LASSO * (1.0 - PRIOR_RELIEF * relief)
        for b in range(mask_ref.shape[1]):
            block = jnp.broadcast_to(row[:, b : b + 1], (BLOCK, BLOCK))
            penalty[b * BLOCK : (b + 1) * BLOCK, h * BLOCK : (h + 1) * BLOCK] = block

    def pair_sum(i):
        x_to = order(i)
        z1_copy(x_to).wait_recv()
        own = part[z_lo * HOPS + x_to, :Z_ROWS].astype(jnp.float32)
        value = own + z1[x_to].astype(jnp.float32)
        zs[x_to] = value.astype(jnp.bfloat16)
        if i == 0:
            r2_copy(0).start()
            r2_copy(1).start()
        elif i < HOPS - 1:
            k = i - 1
            rows = pl.ds(k * half, half)
            r2_copy(k).wait_recv()
            value = zs[x_to, rows].astype(jnp.float32) + r2[k].astype(jnp.float32)
            zs[x_to, rows] = value.astype(jnp.bfloat16)
            x2_copy(k).start()

    value = gram_mid[x_at].astype(jnp.float32)
    for slot in xs_at:
        gx_copy(x_at, slot).wait_recv()
        value = value + gram_x[slot].astype(jnp.float32)
    gram[z_hi, y_at, core, cell] = value.astype(jnp.bfloat16)
    for x_to in xs_at:
        hx_copy(x_to, x_at).start()
    r1_copy(1).start()
    pass_on(0)
    pair_sum(0)
    x1_copy(z_lo, 0).start()

    for slot in xs_at:
        hx_copy(x_at, slot).wait_recv()
    hz_copy(z_lo).start()
    for i in range(2, HOPS):
        z1_copy(order(i)).start()

    hz_copy(1 - z_lo).wait_recv()
    spread = Spread(
        gram, (z_hi, y_at, core), slice(0, HOPS), slice(HOPS, pieces),
        [(y_to, {"cell": cell, "gene": z_hi * 8 + y_to * 2 + core}) for y_to in ys_at],
        {"cell": across[0], "gene": across[1]}, {"cell": cell, "gene": core_partner},
        (gy_send, gy_recv, ga_send, ga_recv, own_send, own_recv),
        (fy_send, fy_recv, fz_send, fz_recv),
    )
    spread.begin()
    pass_on(1)
    spread.relay_high()
    pair_sum(1)
    pair_sum(2)

    value = part[(1 - z_lo) * HOPS + x_at, Z_ROWS:].astype(jnp.float32)
    for k in range(2):
        x1_copy(1 - z_lo, k).wait_recv()
        value = value + x1[1 - z_lo, k].astype(jnp.float32)
    xs[...] = value.astype(jnp.bfloat16)
    z2_copy().start()
    spread.relay_low()
    pair_sum(3)

    for o in range(1, cells):
        sq_copy(cell, (cell + o) % cells).wait_recv()
    sum_squares = jnp.sum(jnp.sum(squares[...], axis=0), keepdims=True)
    total_cells = cells * x.shape[1]
    step_size = 0.5 / (sum_squares / (total_cells * factors) + EPSILON)
    scale = step_size / total_cells
    inverse = 1.0 / (1.0 + step_size * RIDGE)

    def shrunk(moved, rows):
        limit = step_size * penalty[rows]
        return (jnp.maximum(moved - limit, 0.0) - jnp.maximum(-moved - limit, 0.0)) * inverse

    def start_from(value, rows):
        first[rows] = value
        start = shrunk(scale * value, rows)
        coef[rows] = start
        coef_bf[rows] = start.astype(jnp.bfloat16)

    for k in range(2):
        x2_copy(k).wait_recv()
        x1_copy(z_lo, k).wait_recv()

    def z_block(b, carry):
        rows = pl.ds(pl.multiple_of(b * BLOCK, BLOCK), BLOCK)
        value = zs[x_at, rows].astype(jnp.float32)
        for k in range(2):
            value = value + x2[k, rows].astype(jnp.float32)
        start_from(value, rows)
        return carry

    lax.fori_loop(0, Z_ROWS // BLOCK, z_block, 0)
    z2_copy().wait_recv()

    def x_block(b, carry):
        low = pl.ds(pl.multiple_of(b * BLOCK, BLOCK), BLOCK)
        rows = pl.ds(pl.multiple_of(b * BLOCK + Z_ROWS, BLOCK), BLOCK)
        value = part[cell, rows].astype(jnp.float32) + z2[low].astype(jnp.float32)
        for k in range(2):
            value = value + x1[z_lo, k, low].astype(jnp.float32)
        start_from(value, rows)
        return carry

    lax.fori_loop(0, (factors - Z_ROWS) // BLOCK, x_block, 0)

    spread.finish()
    height = out_ref.shape[0]

    def out_copy(t, slot):
        lanes = pl.ds(pl.multiple_of(slot * width, width), width)
        return remote(sent.at[t], out_ref.at[:, lanes], out_send.at[t], out_recv.at[slot], t, gene)

    def finish(i, carry):
        p = (cell // 2 + 1 + i) % HOPS
        rows = pl.ds(pl.multiple_of(p * (2 * height), 64), 2 * height)
        block = gram[p // 2, pl.ds(p % 2 * 2, 2), :, :pieces].reshape(2 * height, factors)
        second = jnp.dot(block, coef_bf[...], preferred_element_type=jnp.float32)
        moved = coef[rows] - scale * (second - first[rows])
        value = (shrunk(moved, rows) * OUT_UNITS).astype(jnp.bfloat16)
        for h in range(2):
            t = 2 * p + h
            piece = value[h * height : (h + 1) * height]

            @pl.when(t != cell)
            def _():
                sent[t] = piece
                out_copy(t, cell).start()

            @pl.when(t == cell)
            def _():
                out_ref[:, pl.ds(pl.multiple_of(cell * width, width), width)] = piece

        return carry

    lax.fori_loop(0, HOPS, finish, 0)

    gz_copy().wait_send()
    hz_copy(z_lo).wait_send()
    for x_to in xs_at:
        gx_copy(x_to, x_at).wait_send()
        hx_copy(x_to, x_at).wait_send()
    spread.drain()

    for x_to in range(HOPS):
        z1_copy(x_to).wait_send()
    for k in range(2):
        r1_copy(k).wait_send()
        r2_copy(k).wait_send()
        x2_copy(k).wait_send()
        for z_to in range(2):
            x1_copy(z_to, k).wait_send()
    z2_copy().wait_send()
    for o in range(1, cells):
        t = (cell + o) % cells
        sq_copy(t, cell).wait_send()
        out_copy(t, cell).wait_send()
        out_copy(cell, t).wait_recv()


def solve(activity_t, expression, block_mask):
    cell_devices, gene_devices = lax.axis_size("cell"), lax.axis_size("gene")
    own, cells = activity_t.shape[-2:]
    factors = gene_devices * own
    width = CHUNK
    rest = factors - Z_ROWS
    bf, f32 = jnp.bfloat16, jnp.float32
    vmem, dma = pltpu.VMEM, pltpu.SemaphoreType.DMA
    return pl.pallas_call(
        solve_kernel,
        out_shape=jax.ShapeDtypeStruct((factors // cell_devices, cell_devices * width), bf),
        in_specs=[
            pl.BlockSpec(memory_space=pl.ANY),
            pl.BlockSpec(memory_space=pl.ANY),
            pl.BlockSpec(memory_space=pltpu.VMEM),
        ],
        out_specs=pl.BlockSpec(memory_space=pltpu.VMEM),
        scratch_shapes=[
            vmem(activity_t.shape, bf),
            vmem((cell_devices, cells, width), bf),
            vmem((cell_devices, factors, width), bf),
            vmem((HOPS, Z_ROWS, width), bf),
            vmem((HOPS, Z_ROWS, width), bf),
            vmem((2, rest, width), bf),
            vmem((2, 2, rest, width), bf),
            vmem((2, Z_ROWS // 2, width), bf),
            vmem((2, Z_ROWS, width), bf),
            vmem((rest, width), bf),
            vmem((rest, width), bf),
            vmem((cell_devices, 16, factors), bf),
            vmem((HOPS, 16, factors), bf),
            vmem((HOPS, 16, factors), bf),
            vmem((HOPS, 16, factors), bf),
            vmem((2, 4, 2, cell_devices, 16, factors), bf),
            vmem((cell_devices, 8, cells), f32),
            vmem((factors, width), f32),
            vmem((factors, width), f32),
            vmem((factors, width), f32),
            vmem((factors, width), bf),
            vmem((cell_devices, factors // cell_devices, width), bf),
            dma, dma((cell_devices,)),
            dma((HOPS,)), dma((HOPS,)),
            dma((2,)), dma((2,)), dma((2, 2)), dma((2, 2)),
            dma((2,)), dma((2,)), dma((2,)), dma((2,)),
            dma, dma,
            dma, dma, dma((HOPS,)), dma((HOPS,)), dma((HOPS,)), dma((HOPS,)), dma, dma,
            dma((2, 4)), dma((2, 4)), dma((2,)), dma((2,)), dma, dma,
            dma((2, 4)), dma((2, 4)), dma((2,)), dma((2,)),
            dma((cell_devices,)), dma((cell_devices,)),
            dma((cell_devices,)), dma((cell_devices,)),
        ],
        compiler_params=pltpu.CompilerParams(
            collective_id=1, has_side_effects=True, vmem_limit_bytes=60 * 2**20
        ),
        name="solve",
    )(activity_t, expression, block_mask)


def on_device(expression, prior_values, block_mask, gram_inverse):
    activity_t = activity_of(expression, prior_values, block_mask, gram_inverse)
    rows = solve(activity_t, expression, block_mask)
    return rows[:, : expression.shape[1]].astype(jnp.float32)


def solution(mesh):
    in_specs = (P("cell", "gene"), P("gene", None), P("gene", None), P(None, "gene"))
    out_specs = P("cell", "gene")
    return jax.shard_map(
        on_device, mesh=mesh, in_specs=in_specs, out_specs=out_specs, check_vma=False
    )
```
